256 devices in a mesh: seq: 16 (over x, y), dp: 8 (over z), head: 2 (over core).
Axes of the slice: x: 4, y: 4, z: 8, core: 2. Of those that a mesh axis runs over, the one named last changes fastest.
Arguments:
- queries: bfloat16 [8, 4096, 2048], P('dp', 'seq', 'head'), may hold values from -40 to 40
- out_grad: bfloat16 [8, 4096, 2048], P('dp', 'seq', 'head'), may hold values from -96 to 96
- encodings: bfloat16 [8, 16384, 896], P('dp', 'seq'), may hold values from -6 to 6
- owner_map: int32 [8, 64, 2], P('dp', 'seq'), may hold values from 0 to 127, as said below
- nbr_count: int32 [8, 64], P('dp', 'seq'), may hold values from 1 to 2
- key_weight: bfloat16 [896, 2048], P(None, 'head'), may hold values from -1 to 1
- value_weight: bfloat16 [896, 2048], P(None, 'head'), may hold values from -0.1875 to 0.1875
Outputs:
- grad_query: bfloat16 [8, 4096, 2048], P('dp', 'seq', 'head')
- grad_enc: bfloat16 [8, 16384, 896], P('dp', 'seq')
- grad_kv_weight: float32 [896, 2, 2048], P(('seq', 'dp'), None, 'head')
The draws below stay inside these ranges and needn't reach their ends.
Inputs may be any that keep to these rules, and one draw needn't show every extreme that they name: `owner_map`: an entry e names the neighbour at place e % 8 on the device with index e // 8 along seq that holds the same sequence. Among the 8 references of the spans of one device, each device along seq is named either by none or by exactly 1 of them.
All inputs are finite; a program needn't handle non-finite values.
Results may differ from the reference program's by a relative error of at most 0.023.
The reference program's roundings to bfloat16 on the way count: a program that leaves them out, or rounds other values in their place, can miss the bound.
Values may be sent and summed in bfloat16 or wider, within the bound.
A program may use at most 128 MiB of HBM per device.

```python
import math
import jax
import jax.numpy as jnp
from jax import lax

HEADS = 16
HD = 128
D_ENC = 896
SPAN = 64
NBR = 2
NROWS = 128
SPAN_DEV = 4
HF = 2048
OWN_DEV = 8
CAP = 1
SEQS = 8
SPANS = 64
LEN = 4096
NEIGH_ROWS = 16384
N_SEQ = 16


def shared_key_weight(key):
    values = jax.random.normal(jax.random.fold_in(key, 103), (D_ENC, HF), jnp.float32) / math.sqrt(D_ENC)
    return jnp.clip(values, -0.9, 0.9)


def draw_key_weight(key, part):
    return shared_key_weight(key).astype(jnp.bfloat16)


def draw_queries(key, part):
    base_key = jax.random.fold_in(key, 107)
    values = jnp.clip(jax.random.normal(base_key, (SEQS, LEN, HF), jnp.float32), -6.0, 6.0)
    return values.astype(jnp.bfloat16)


def draw_encodings(key, part):
    base_key = jax.random.fold_in(key, 113)
    values = jnp.clip(jax.random.normal(base_key, (SEQS, NEIGH_ROWS, D_ENC), jnp.float32), -6.0, 6.0)
    return values.astype(jnp.bfloat16)


def draw_owner_map(key, part):
    blocks = SEQS * N_SEQ
    block_refs = NBR * SPAN_DEV
    groups = block_refs // CAP
    holder_numbers = jnp.arange(N_SEQ, dtype=jnp.int32)
    logit_scores = jax.random.randint(jax.random.fold_in(key, 121), (blocks, N_SEQ), 0, 2 ** 16, jnp.int32)
    popular_ranking = jax.random.permutation(jax.random.fold_in(key, 122), N_SEQ)
    extra_credit = (popular_ranking < max(1, N_SEQ // 4)).astype(jnp.int32) * 2 ** 15
    block_index = jnp.arange(blocks, dtype=jnp.int32) % N_SEQ
    required_picks = jnp.logical_and((block_index == 0)[:, None], (holder_numbers == N_SEQ - 1)[None, :]).astype(jnp.int32) * 2 ** 17
    running_totals = (logit_scores + extra_credit[None, :] + required_picks) * N_SEQ + holder_numbers[None, :]
    unused, chosen = lax.top_k(running_totals, groups)
    owners = jnp.repeat(chosen.astype(jnp.int32), CAP, axis=1)
    places = jax.random.randint(jax.random.fold_in(key, 123), (blocks, block_refs), 0, OWN_DEV, jnp.int32)
    first_ref = jnp.logical_and((block_index == 0)[:, None], (jnp.arange(block_refs) == 0)[None, :])
    places = jnp.where(first_ref, OWN_DEV - 1, places)
    shuffle_keys = jax.random.randint(jax.random.fold_in(key, 124), (blocks, block_refs), 0, 2 ** 20, jnp.int32) * block_refs + jnp.arange(block_refs, dtype=jnp.int32)[None, :]
    order = jnp.argsort(shuffle_keys, axis=1, stable=True)
    owners = jnp.take_along_axis(owners, order, axis=1)
    places = jnp.take_along_axis(places, order, axis=1)
    return (owners * OWN_DEV + places).reshape(SEQS, SPANS, NBR).astype(jnp.int32)


def touch_ends(array, own_key, smallest, high):
    longest = array.shape.index(max(array.shape))
    spots = []
    for shift in (0, 1):
        where = [jax.random.randint(jax.random.fold_in(own_key, axis), (), 0, length) for axis, length in enumerate(array.shape)]
        where[longest] = (where[longest] + shift) % array.shape[longest]
        spots.append(tuple(where))
    return array.at[spots[0]].set(smallest).at[spots[1]].set(high)


def shard_levels(rng, extent, pieces, smallest, largest):
    gain, own = 1.0, jax.random.fold_in(rng, 6)
    for dim, parts in pieces:
        draws = jnp.exp(jax.random.uniform(jax.random.fold_in(own, dim), (parts,), jnp.float32, smallest / len(pieces), largest / len(pieces)))
        gain = gain * jnp.repeat(draws, extent[dim] // parts).reshape([-1 if axis == dim else 1 for axis in range(len(extent))])
    return gain


def scatter_about(rng, shape, width, bound, pieces=(), kind=jnp.bfloat16):
    gain = shard_levels(rng, shape, pieces, -0.22, 0.18) if pieces else 1.0
    array = jax.random.normal(rng, shape, jnp.float32) * width * gain
    return jnp.minimum(jnp.maximum(array, -bound), bound).astype(kind)


def setup_inputs(seed: int = 0) -> dict:
    keys = jax.random.split(jax.random.key(seed), 8)
    return {
        "queries": draw_queries(jax.random.fold_in(keys[7], 71), 0),
        "out_grad": scatter_about(keys[1], (SEQS, LEN, HF), 16.0, 96.0, ((0, 8), (1, 16), (2, 2))),
        "encodings": draw_encodings(jax.random.fold_in(keys[7], 71), 0),
        "owner_map": draw_owner_map(jax.random.fold_in(keys[7], 71), 0),
        "nbr_count": touch_ends(jax.random.randint(keys[4], (SEQS, SPANS), 1, 3), jax.random.fold_in(keys[4], 1), 1, 2).astype(jnp.int32),
        "key_weight": draw_key_weight(jax.random.fold_in(keys[7], 71), 0),
        "value_weight": scatter_about(keys[6], (D_ENC, HF), D_ENC ** -0.5, 0.1875, ((1, 2),)),
    }


def reference(queries, out_grad, encodings, owner_map, nbr_count, key_weight, value_weight):
    score_scale = 1.0 / math.sqrt(HD)
    neighbours = N_SEQ * OWN_DEV
    rim_rows = SPAN - 1
    key_wide_w = key_weight.astype(jnp.float32)
    value_wide_w = value_weight.astype(jnp.float32)

    def one_sequence(carry, items):
        seq_query, seq_grad, seq_enc, seq_map, seq_count = items
        keys_all = jnp.dot(seq_enc, key_weight, preferred_element_type=jnp.float32).astype(jnp.bfloat16).reshape(neighbours, NROWS, HF)
        values_all = jnp.dot(seq_enc, value_weight, preferred_element_type=jnp.float32).astype(jnp.bfloat16).reshape(neighbours, NROWS, HF)
        padding = jnp.zeros((rim_rows, HF), jnp.bfloat16)
        shifted_query = jnp.concatenate([seq_query[rim_rows:], padding], axis=0)
        shifted_grad = jnp.concatenate([seq_grad[rim_rows:], padding], axis=0)
        chosen = seq_map.reshape(SPANS * NBR).astype(jnp.int32)
        context_keys = keys_all[chosen].reshape(SPANS, NBR * NROWS, HEADS, HD)
        context_values = values_all[chosen].reshape(SPANS, NBR * NROWS, HEADS, HD)
        query_blocks = shifted_query.reshape(SPANS, SPAN, HEADS, HD)
        grad_blocks = shifted_grad.reshape(SPANS, SPAN, HEADS, HD)
        query_wide = query_blocks.astype(jnp.float32)
        grad_wide = grad_blocks.astype(jnp.float32)
        keys_wide = context_keys.astype(jnp.float32)
        values_wide = context_values.astype(jnp.float32)
        allowed = (jnp.arange(NBR * NROWS) // NROWS)[None, :] < seq_count[:, None]
        logit_scores = jnp.einsum('cqhd,ckhd->chqk', query_wide, keys_wide) * score_scale
        logit_scores = jnp.where(allowed[:, None, None, :], logit_scores, -1e+30)
        row_max = lax.optimization_barrier(jnp.max(logit_scores, axis=-1, keepdims=True))
        weights = jnp.exp(logit_scores - row_max)
        softmax_p = weights / lax.optimization_barrier(jnp.sum(weights, axis=-1, keepdims=True))
        prob_bf = softmax_p.astype(jnp.bfloat16)
        prob_wide = prob_bf.astype(jnp.float32)
        attended = jnp.einsum('chqk,ckhd->cqhd', prob_wide, values_wide)
        row_delta = lax.optimization_barrier(jnp.sum(grad_wide * attended, axis=-1))
        dprobs = jnp.einsum('cqhd,ckhd->chqk', grad_wide, values_wide)
        dscores = softmax_p * (dprobs - jnp.transpose(row_delta, (0, 2, 1))[..., None])
        dscore_wide = dscores.astype(jnp.bfloat16).astype(jnp.float32)
        gradient_offset = (jnp.einsum('chqk,ckhd->cqhd', dscore_wide, keys_wide) * score_scale).astype(jnp.bfloat16).reshape(LEN, HF)
        grad_rows = jnp.concatenate([padding, gradient_offset[:LEN - rim_rows]], axis=0)
        ref_key_grad = (jnp.einsum('chqk,cqhd->ckhd', dscore_wide, query_wide) * score_scale).astype(jnp.bfloat16)
        ref_value_grad = jnp.einsum('chqk,cqhd->ckhd', prob_wide, grad_wide).astype(jnp.bfloat16)
        flat_key_grad = ref_key_grad.reshape(SPANS * NBR, NROWS * HF).astype(jnp.float32)
        flat_value_grad = ref_value_grad.reshape(SPANS * NBR, NROWS * HF).astype(jnp.float32)
        summed_keys = jnp.zeros((neighbours, NROWS * HF), jnp.float32).at[chosen].add(flat_key_grad).reshape(neighbours * NROWS, HF)
        summed_values = jnp.zeros((neighbours, NROWS * HF), jnp.float32).at[chosen].add(flat_value_grad).reshape(neighbours * NROWS, HF)
        enc_grad = jnp.dot(summed_keys, key_wide_w.T, precision=lax.Precision.HIGHEST) + jnp.dot(summed_values, value_wide_w.T, precision=lax.Precision.HIGHEST)
        enc_grad = enc_grad.astype(jnp.bfloat16)
        enc_wide = seq_enc.astype(jnp.float32)
        weight_add = jnp.stack([jnp.dot(enc_wide.T, summed_keys, precision=lax.Precision.HIGHEST), jnp.dot(enc_wide.T, summed_values, precision=lax.Precision.HIGHEST)], axis=1)
        return (carry + weight_add, (grad_rows, enc_grad))
    start_weight = jnp.zeros((D_ENC, 2, HF), jnp.float32)
    weight_total, outputs = lax.scan(one_sequence, start_weight, (queries, out_grad, encodings, owner_map, nbr_count))
    return (outputs[0], outputs[1], weight_total)
```

```python
import functools
import math

import jax
import jax.numpy as jnp
from jax import lax
from jax.experimental import pallas as pl
from jax.experimental.pallas import tpu as pltpu
from jax.sharding import PartitionSpec as P

MESH = pl.DeviceIdType.MESH
HD = 128
SPAN = 64
NROWS = 128
REFS = 8
SIDE = 4
PEERS = SIDE * SIDE
DEPTH = 8
HALF = NROWS // 2
OWNED = 8
D_ENC = 896
FEAT = 1024
ROWS = 256
RIM = 64
STEP = 256
VMEM_LIMIT = 58 << 20
BF = jnp.bfloat16
F32 = jnp.float32


def ring(step):
    return min(step, SIDE - step)


STEPS = sorted(
    [(dx, dy) for dx in range(SIDE) for dy in range(SIDE) if (dx, dy) != (0, 0)],
    key=lambda s: -(ring(s[0]) + ring(s[1])),
)


def plane_place():
    me = lax.axis_index("seq")
    return me, lax.div(me, SIDE), lax.rem(me, SIDE)


def shifted_peer(x, y, dx, dy):
    return lax.rem(x + dx, SIDE) * SIDE + lax.rem(y + dy, SIDE)


def remote(src, dst, send_sem, recv_sem, **where):
    return pltpu.make_async_remote_copy(
        src_ref=src,
        dst_ref=dst,
        send_sem=send_sem,
        recv_sem=recv_sem,
        device_id=where,
        device_id_type=MESH,
    )


def greet(barrier, **where):
    pl.semaphore_signal(barrier, inc=1, device_id=where, device_id_type=MESH)


def nt(a, b):
    return lax.dot_general(a, b, (((1,), (1,)), ((), ())), preferred_element_type=F32)


def tn(a, b):
    return lax.dot_general(a, b, (((0,), (0,)), ((), ())), preferred_element_type=F32)


def nn(a, b):
    return jnp.dot(a, b, preferred_element_type=F32)


def shift_matrix(rows, columns, by):
    i = lax.broadcasted_iota(jnp.int32, (rows, columns), 0)
    e = lax.broadcasted_iota(jnp.int32, (rows, columns), 1)
    return (e == i + by).astype(F32).astype(BF)


def fetch_kernel(
    map_ref, enc_ref, q_ref, d_ref,
    slots_ref, hq_ref, hd_ref, tab_ref,
    asked, tabv, send, isend, irecv, ssend, srecv, fsend, frecv, hsend, hrecv, lsem,
):
    me, x, y = plane_place()
    core = lax.axis_index("head")
    other = 1 - core
    barrier = pltpu.get_barrier_semaphore()
    for dx, dy in STEPS:
        greet(barrier, seq=shifted_peer(x, y, dx, dy))
    greet(barrier, head=other)
    lane = lax.broadcasted_iota(jnp.int32, (1, 128), 1)
    row = jnp.zeros((1, 128), jnp.int32)
    for r in range(REFS):
        entry = map_ref[r // 2, r % 2]
        row = jnp.where(lane == entry // OWNED, entry % OWNED + 1, row)
    asked[...] = row
    tabv[me] = row
    pl.semaphore_wait(barrier, PEERS)

    copies = []
    for k, (dx, dy) in enumerate(STEPS):
        c = remote(asked, tabv.at[me], isend.at[k], irecv.at[k], seq=shifted_peer(x, y, dx, dy))
        c.start()
        copies.append(c)
    before = lax.rem(me + PEERS - 1, PEERS)
    halos = [
        remote(q_ref.at[pl.ds(0, RIM)], hq_ref, hsend.at[0], hrecv.at[0], seq=before),
        remote(d_ref.at[pl.ds(0, RIM)], hd_ref, hsend.at[1], hrecv.at[1], seq=before),
    ]
    for c in copies:
        c.wait_recv()
    lc = pltpu.make_async_copy(tabv, tab_ref, lsem)
    lc.start()
    lc.wait()
    mine = pl.ds(pl.multiple_of(core * HALF, HALF), HALF)
    sends = []
    for k, (dx, dy) in enumerate(STEPS):
        peer = shifted_peer(x, y, dx, dy)
        place = jnp.maximum(tab_ref[peer, 0, me] - 1, 0)
        send[k] = enc_ref[place, mine, :]
        c = remote(send.at[k], slots_ref.at[me, mine], ssend.at[k], srecv.at[k], seq=peer)
        c.start()
        sends.append(c)
    for c in halos:
        c.start()
    slots_ref[me] = enc_ref[jnp.maximum(tab_ref[me, 0, me] - 1, 0)]
    shares = []
    for k in reversed(range(len(STEPS))):
        dx, dy = STEPS[k]
        source = shifted_peer(x, y, SIDE - dx, SIDE - dy)
        sends[k].wait_recv()
        half = slots_ref.at[source, mine]
        c = remote(half, half, fsend.at[k], frecv.at[k], head=other)
        c.start()
        shares.append(c)
    for c in copies:
        c.wait_send()
    for c in halos:
        c.wait()
    for c in sends:
        c.wait_send()
    for c in shares:
        c.wait()


def span_kernel(
    map_ref, cnt_ref, slots_ref, wk_ref, wv_ref, q_ref, d_ref, hq_ref, hd_ref,
    gs_ref, dw_ref, con_ref,
    refs, refs_t, kbuf, vbuf, dkbuf, dvbuf,
):
    scale = 1.0 / math.sqrt(HD)
    step = pl.program_id(0)
    last = lax.axis_index("seq") == PEERS - 1

    @pl.when(step == 0)
    def _():
        for r in range(REFS):
            block = slots_ref[map_ref[r // 2, r % 2] // OWNED]
            refs[pl.ds(r * NROWS, NROWS), :] = block
            refs_t[:, pl.ds(r * NROWS, NROWS)] = block.T
        con_ref[...] = jnp.zeros_like(con_ref)

    wk = wk_ref[...]
    wv = wv_ref[...]
    kbuf[...] = nn(refs[...], wk).astype(BF)
    vbuf[...] = nn(refs[...], wv).astype(BF)
    move = shift_matrix(ROWS, ROWS + RIM, RIM - 1)
    keep = jnp.where(last, 0.0, 1.0).astype(BF)
    qs = nn(move, jnp.concatenate([q_ref[...], hq_ref[...] * keep], axis=0)).astype(BF)
    do = nn(move, jnp.concatenate([d_ref[...], hd_ref[...] * keep], axis=0)).astype(BF)
    col = lax.broadcasted_iota(jnp.int32, (SPAN, 2 * NROWS), 1)
    units = [(c, h) for c in range(REFS // 2) for h in range(STEP // HD)]

    def cut(a, c, h, n):
        return a[c * n : (c + 1) * n, h * HD : (h + 1) * HD]

    keys = [kbuf[pl.ds(c * 2 * NROWS, 2 * NROWS), pl.ds(h * HD, HD)] for c, h in units]
    vals = [vbuf[pl.ds(c * 2 * NROWS, 2 * NROWS), pl.ds(h * HD, HD)] for c, h in units]
    q_u = [cut(qs, c, h, SPAN) for c, h in units]
    d_u = [cut(do, c, h, SPAN) for c, h in units]
    scores = [nt(q, k) * scale for q, k in zip(q_u, keys)]
    dprobs = [nt(d, v) for d, v in zip(d_u, vals)]
    probs, probs_b, ds_b = [], [], []
    for (c, h), s, dp in zip(units, scores, dprobs):
        s = jnp.where(col < cnt_ref[0, c] * NROWS, s, -1e30)
        w = jnp.exp(s - jnp.max(s, axis=-1, keepdims=True))
        p = w / jnp.sum(w, axis=-1, keepdims=True)
        pb = p.astype(BF)
        delta = jnp.sum(pb.astype(F32) * dp, axis=-1, keepdims=True)
        probs_b.append(pb)
        ds_b.append((p * (dp - delta)).astype(BF))
    for (c, h), q, d, k, pb, ds in zip(units, q_u, d_u, keys, probs_b, ds_b):
        at = (pl.ds(c * 2 * NROWS, 2 * NROWS), pl.ds(h * HD, HD))
        gs_ref[pl.ds(c * SPAN, SPAN), pl.ds(h * HD, HD)] = (nn(ds, k) * scale).astype(BF)
        dkbuf[at] = (tn(ds, q) * scale).astype(BF)
        dvbuf[at] = tn(pb, d).astype(BF)
    dw_ref[0] = nn(refs_t[...], dkbuf[...]).astype(BF).reshape(PEERS, D_ENC // PEERS, STEP)
    dw_ref[1] = nn(refs_t[...], dvbuf[...]).astype(BF).reshape(PEERS, D_ENC // PEERS, STEP)
    con_ref[...] += nt(dkbuf[...], wk) + nt(dvbuf[...], wv)


def give_kernel(
    map_ref, tab_ref, con_ref, dw_ref, gs_ref,
    gq_ref, ge_ref, gw_ref,
    hbuf, half, send, recv, ohalf, prev, r1a, r1b, s2a, s2b, r2a, r2b, s3, r3,
    hsem, ssend, srecv, osem, psem, send1a, recv1a, send1b, recv1b,
    send2a, recv2a, send2b, recv2b, send3, recv3,
):
    me, x, y = plane_place()
    core = lax.axis_index("head")
    level = lax.axis_index("dp")
    other = 1 - core
    barrier = pltpu.get_barrier_semaphore()
    for dx, dy in STEPS:
        greet(barrier, seq=shifted_peer(x, y, dx, dy))
    greet(barrier, head=other)
    for dz in range(1, DEPTH):
        greet(barrier, dp=lax.rem(level + dz, DEPTH))
    pl.semaphore_wait(barrier, PEERS + DEPTH - 1)

    mine = pl.ds(pl.multiple_of(core * HALF, HALF), HALF)
    theirs = pl.ds(pl.multiple_of(other * HALF, HALF), HALF)
    swap = remote(con_ref.at[:, theirs], hbuf, hsem.at[0], hsem.at[1], head=other)
    swap.start()
    after = lax.rem(me + 1, PEERS)
    halo = remote(gs_ref.at[pl.ds(ROWS - RIM, RIM)], prev, psem.at[0], psem.at[1], seq=after)
    halo.start()
    first_a, first_b = [], []
    for k in (2, 1, 3):
        xp = lax.rem(x + k, SIDE)
        yp = lax.rem(y + k, SIDE)
        ca = remote(dw_ref.at[0, xp], r1a.at[k - 1], send1a.at[k - 1], recv1a.at[k - 1], seq=xp * SIDE + y)
        cb = remote(dw_ref.at[1, :, yp], r1b.at[k - 1], send1b.at[k - 1], recv1b.at[k - 1], seq=x * SIDE + yp)
        ca.start()
        cb.start()
        first_a.append(ca)
        first_b.append(cb)

    swap.wait()
    for r in range(REFS):
        half[r] = (con_ref[r, mine, :] + hbuf[r]).astype(BF)
    owners = [map_ref[r // 2, r % 2] // OWNED for r in range(REFS)]

    def ref_for(peer):
        found = jnp.int32(0)
        for r in range(REFS):
            found = jnp.where(owners[r] == peer, jnp.int32(r), found)
        return found

    sends = []
    for k, (dx, dy) in enumerate(STEPS):
        peer = shifted_peer(x, y, dx, dy)
        send[k] = half[ref_for(peer)]
        c = remote(send.at[k], recv.at[me], ssend.at[k], srecv.at[k], seq=peer)
        c.start()
        sends.append(c)
    recv[me] = half[ref_for(me)]

    for c in first_a:
        c.wait()
    for c in first_b:
        c.wait()

    def up(a):
        return a.astype(F32)

    for j in range(SIDE):
        s2a[j] = (up(dw_ref[0, x, j]) + up(r1a[0, j]) + up(r1a[1, j]) + up(r1a[2, j])).astype(BF)
        s2b[j] = (up(dw_ref[1, j, y]) + up(r1b[0, j]) + up(r1b[1, j]) + up(r1b[2, j])).astype(BF)
    second = []
    for k in (2, 1, 3):
        xp = lax.rem(x + k, SIDE)
        yp = lax.rem(y + k, SIDE)
        ca = remote(s2a.at[yp], r2a.at[k - 1], send2a.at[k - 1], recv2a.at[k - 1], seq=x * SIDE + yp)
        cb = remote(s2b.at[xp], r2b.at[k - 1], send2b.at[k - 1], recv2b.at[k - 1], seq=xp * SIDE + y)
        ca.start()
        cb.start()
        second += [ca, cb]

    halo.wait()
    old = jnp.where(me == 0, 0.0, 1.0).astype(BF)
    move = shift_matrix(ROWS, ROWS + RIM, 1)
    gq_ref[...] = nn(move, jnp.concatenate([prev[...] * old, gs_ref[...]], axis=0)).astype(BF)

    for c in second:
        c.wait()
    own_a = up(dw_ref[0, x, y]) + up(r1a[0, y]) + up(r1a[1, y]) + up(r1a[2, y])
    own_b = up(dw_ref[1, x, y]) + up(r1b[0, x]) + up(r1b[1, x]) + up(r1b[2, x])
    t_a = (own_a + up(r2a[0]) + up(r2a[1]) + up(r2a[2])).astype(BF)
    t_b = (own_b + up(r2b[0]) + up(r2b[1]) + up(r2b[2])).astype(BF)
    rows = D_ENC // PEERS
    piece = rows // DEPTH
    m = lax.broadcasted_iota(jnp.int32, (DEPTH * 8, rows), 0)
    e = lax.broadcasted_iota(jnp.int32, (DEPTH * 8, rows), 1)
    spread = jnp.logical_and(m // 8 * piece + m % 8 == e, m % 8 < piece).astype(F32).astype(BF)
    s3[:, 0] = nn(spread, t_a).astype(BF).reshape(DEPTH, 8, FEAT)
    s3[:, 1] = nn(spread, t_b).astype(BF).reshape(DEPTH, 8, FEAT)
    third = []
    for dz in (4, 3, 5, 2, 6, 1, 7):
        zp = lax.rem(level + dz, DEPTH)
        c = remote(s3.at[zp], r3.at[dz - 1], send3.at[dz - 1], recv3.at[dz - 1], dp=zp)
        c.start()
        third.append(c)

    for c in sends:
        c.wait()
    row = lax.broadcasted_iota(jnp.int32, (OWNED * HALF, 2 * HALF), 0)
    lane = lax.broadcasted_iota(jnp.int32, (OWNED * HALF, 2 * HALF), 1)
    pick = []
    for t in range(PEERS // 2):
        lo = (tab_ref[2 * t, 0, me] - 1) * HALF
        hi = (tab_ref[2 * t + 1, 0, me] - 1) * HALF
        target = jnp.where(lane < HALF, lane + lo, lane - HALF + hi)
        live = jnp.where(lane < HALF, lo, hi) >= 0
        pick.append(jnp.logical_and(row == target, live).astype(F32).astype(BF))
    total = nn(jnp.concatenate(pick, axis=1), recv[...].reshape(PEERS * HALF, D_ENC))
    total = total.astype(BF).reshape(OWNED, HALF, D_ENC)
    ohalf[...] = total
    ge_ref[:, mine, :] = total
    back = remote(ohalf, ge_ref.at[:, mine], osem.at[0], osem.at[1], head=other)
    back.start()

    for c in third:
        c.wait()
    final = up(s3[level])
    for k in range(DEPTH - 1):
        final = final + up(r3[k])
    gw_ref[:, 0, :] = final[0, :piece]
    gw_ref[:, 1, :] = final[1, :piece]
    back.wait()


def body(queries, out_grad, encodings, owner_map, nbr_count, key_weight, value_weight):
    vm = pl.BlockSpec(memory_space=pltpu.VMEM)
    sm = pl.BlockSpec(memory_space=pltpu.SMEM)
    dma = pltpu.SemaphoreType.DMA
    n = len(STEPS)
    enc = encodings.reshape(OWNED, NROWS, D_ENC)
    q, d = queries[0], out_grad[0]
    slots, hq, hd, tab = pl.pallas_call(
        fetch_kernel,
        out_shape=(
            jax.ShapeDtypeStruct((PEERS, NROWS, D_ENC), BF),
            jax.ShapeDtypeStruct((RIM, FEAT), BF),
            jax.ShapeDtypeStruct((RIM, FEAT), BF),
            jax.ShapeDtypeStruct((PEERS, 1, 128), jnp.int32),
        ),
        in_specs=[sm, vm, vm, vm],
        out_specs=(vm, vm, vm, sm),
        scratch_shapes=[
            pltpu.VMEM((1, 128), jnp.int32),
            pltpu.VMEM((PEERS, 1, 128), jnp.int32),
            pltpu.VMEM((n, HALF, D_ENC), BF),
            dma((n,)), dma((n,)), dma((n,)), dma((n,)), dma((n,)), dma((n,)),
            dma((2,)), dma((2,)), dma,
        ],
        compiler_params=pltpu.CompilerParams(
            collective_id=0, has_side_effects=True, vmem_limit_bytes=VMEM_LIMIT
        ),
        name="fetch",
    )(owner_map[0], enc, q, d)

    rows = D_ENC // PEERS
    gs, dw, con = pl.pallas_call(
        span_kernel,
        grid=(FEAT // STEP,),
        out_shape=(
            jax.ShapeDtypeStruct((ROWS, FEAT), BF),
            jax.ShapeDtypeStruct((2, PEERS, rows, FEAT), BF),
            jax.ShapeDtypeStruct((REFS * NROWS, D_ENC), F32),
        ),
        in_specs=[
            sm, sm,
            pl.BlockSpec((PEERS, NROWS, D_ENC), lambda g: (0, 0, 0)),
            pl.BlockSpec((D_ENC, STEP), lambda g: (0, g)),
            pl.BlockSpec((D_ENC, STEP), lambda g: (0, g)),
            pl.BlockSpec((ROWS, STEP), lambda g: (0, g)),
            pl.BlockSpec((ROWS, STEP), lambda g: (0, g)),
            pl.BlockSpec((RIM, STEP), lambda g: (0, g)),
            pl.BlockSpec((RIM, STEP), lambda g: (0, g)),
        ],
        out_specs=(
            pl.BlockSpec((ROWS, STEP), lambda g: (0, g)),
            pl.BlockSpec((2, PEERS, rows, STEP), lambda g: (0, 0, 0, g)),
            pl.BlockSpec((REFS * NROWS, D_ENC), lambda g: (0, 0)),
        ),
        scratch_shapes=[
            pltpu.VMEM((REFS * NROWS, D_ENC), BF),
            pltpu.VMEM((D_ENC, REFS * NROWS), BF),
            pltpu.VMEM((REFS * NROWS, STEP), BF),
            pltpu.VMEM((REFS * NROWS, STEP), BF),
            pltpu.VMEM((REFS * NROWS, STEP), BF),
            pltpu.VMEM((REFS * NROWS, STEP), BF),
        ],
        compiler_params=pltpu.CompilerParams(
            dimension_semantics=("arbitrary",), vmem_limit_bytes=VMEM_LIMIT
        ),
        name="spans",
    )(owner_map[0], nbr_count, slots, key_weight, value_weight, q, d, hq, hd)

    gq, ge, gw = pl.pallas_call(
        give_kernel,
        out_shape=(
            jax.ShapeDtypeStruct((ROWS, FEAT), BF),
            jax.ShapeDtypeStruct((OWNED, NROWS, D_ENC), BF),
            jax.ShapeDtypeStruct((rows // DEPTH, 2, FEAT), F32),
        ),
        in_specs=[sm, sm, vm, vm, vm],
        out_specs=(vm, vm, vm),
        scratch_shapes=[
            pltpu.VMEM((REFS, HALF, D_ENC), F32),
            pltpu.VMEM((REFS, HALF, D_ENC), BF),
            pltpu.VMEM((n, HALF, D_ENC), BF),
            pltpu.VMEM((PEERS, HALF, D_ENC), BF),
            pltpu.VMEM((OWNED, HALF, D_ENC), BF),
            pltpu.VMEM((RIM, FEAT), BF),
            pltpu.VMEM((SIDE - 1, SIDE, rows, FEAT), BF),
            pltpu.VMEM((SIDE - 1, SIDE, rows, FEAT), BF),
            pltpu.VMEM((SIDE, rows, FEAT), BF),
            pltpu.VMEM((SIDE, rows, FEAT), BF),
            pltpu.VMEM((SIDE - 1, rows, FEAT), BF),
            pltpu.VMEM((SIDE - 1, rows, FEAT), BF),
            pltpu.VMEM((DEPTH, 2, 8, FEAT), BF),
            pltpu.VMEM((DEPTH - 1, 2, 8, FEAT), BF),
            dma((2,)), dma((n,)), dma((n,)), dma((2,)), dma((2,)),
            dma((3,)), dma((3,)), dma((3,)), dma((3,)),
            dma((3,)), dma((3,)), dma((3,)), dma((3,)),
            dma((DEPTH - 1,)), dma((DEPTH - 1,)),
        ],
        compiler_params=pltpu.CompilerParams(
            collective_id=1, has_side_effects=True, vmem_limit_bytes=VMEM_LIMIT
        ),
        name="give",
    )(
        owner_map[0], tab, con.reshape(REFS, NROWS, D_ENC),
        dw.reshape(2, SIDE, SIDE, rows, FEAT), gs,
    )
    return gq[None], ge.reshape(1, OWNED * NROWS, D_ENC), gw


def solution(mesh):
    return jax.shard_map(
        body,
        mesh=mesh,
        in_specs=(
            P("dp", "seq", "head"),
            P("dp", "seq", "head"),
            P("dp", "seq", None),
            P("dp", "seq", None),
            P("dp", "seq"),
            P(None, "head"),
            P(None, "head"),
        ),
        out_specs=(P("dp", "seq", "head"), P("dp", "seq", None), P(("seq", "dp"), None, "head")),
        check_vma=False,
    )
```

```python
import functools
import math

import jax
import jax.numpy as jnp
from jax import lax
from jax.experimental import pallas as pl
from jax.experimental.pallas import tpu as pltpu
from jax.sharding import PartitionSpec as P

MESH = pl.DeviceIdType.MESH
HD = 128
SPAN = 64
NROWS = 128
REFS = 8
SIDE = 4
PEERS = SIDE * SIDE
DEPTH = 8
HALF = NROWS // 2
OWNED = 8
D_ENC = 896
FEAT = 1024
ROWS = 256
RIM = 64
STEP = 256
GROUPS = FEAT // STEP
SHARE = D_ENC // PEERS
PIECE = SHARE // DEPTH
VMEM_LIMIT = 58 << 20
BF = jnp.bfloat16
F32 = jnp.float32


def plane_place():
    me = lax.axis_index("seq")
    return me, lax.div(me, SIDE), lax.rem(me, SIDE)


def plane_peer(x, y, k):
    return lax.rem(x + lax.div(k, SIDE), SIDE) * SIDE + lax.rem(y + lax.rem(k, SIDE), SIDE)


def opposite(k):
    return lax.rem(SIDE - lax.div(k, SIDE), SIDE) * SIDE + lax.rem(SIDE - lax.rem(k, SIDE), SIDE)


def each(start, stop, step):
    def one(k, carry):
        step(k)
        return carry

    lax.fori_loop(start, stop, one, 0)


def up(a):
    return a.astype(F32)


def remote(src, dst, send_sem, recv_sem, **where):
    return pltpu.make_async_remote_copy(
        src_ref=src,
        dst_ref=dst,
        send_sem=send_sem,
        recv_sem=recv_sem,
        device_id=where,
        device_id_type=MESH,
    )


def greet(barrier, **where):
    pl.semaphore_signal(barrier, inc=1, device_id=where, device_id_type=MESH)


def nt(a, b):
    return lax.dot_general(a, b, (((1,), (1,)), ((), ())), preferred_element_type=F32)


def tn(a, b):
    return lax.dot_general(a, b, (((0,), (0,)), ((), ())), preferred_element_type=F32)


def nn(a, b):
    return jnp.dot(a, b, preferred_element_type=F32)


def shift_matrix(rows, columns, by):
    i = lax.broadcasted_iota(jnp.int32, (rows, columns), 0)
    e = lax.broadcasted_iota(jnp.int32, (rows, columns), 1)
    return (e == i + by).astype(F32).astype(BF)


def kernel(
    map_ref, cnt_ref, enc_hbm, q_hbm, d_hbm, wk_hbm, wv_hbm,
    gq_hbm, ge_hbm, gw_ref,
    enc, wk, wv, qx, dx, asked, tabv, tab, send, slots, keys, vals, enct, refs_t,
    dk, dv, con, hbuf, half, recv, ohalf, gs, prev, gqv, dw, r1a, r1b, s2a, s2b, r2a, r2b, s3, r3,
    lsem, osem, isend, irecv, ssend, srecv, fsend, frecv, halo_send, halo_recv,
    swap_sem, rsend, rrecv, back_sem, prev_sem,
    send1a, recv1a, send1b, recv1b, send2a, recv2a, send2b, recv2b, send3, recv3,
):
    me, x, y = plane_place()
    core = lax.axis_index("head")
    level = lax.axis_index("dp")
    other = 1 - core
    scale = 1.0 / math.sqrt(HD)
    mine = pl.ds(pl.multiple_of(core * HALF, HALF), HALF)
    theirs = pl.ds(pl.multiple_of(other * HALF, HALF), HALF)

    barrier = pltpu.get_barrier_semaphore()
    each(1, PEERS, lambda k: greet(barrier, seq=plane_peer(x, y, k)))
    greet(barrier, head=other)
    each(1, DEPTH, lambda k: greet(barrier, dp=lax.rem(level + k, DEPTH)))

    enc_load = pltpu.make_async_copy(enc_hbm, enc, lsem.at[0])
    enc_load.start()
    loads = []
    for g in range(GROUPS):
        cols = pl.ds(g * STEP, STEP)
        loads.append(pltpu.make_async_copy(q_hbm.at[:, cols], qx.at[g, pl.ds(0, ROWS)], lsem.at[1 + g]))
        loads.append(pltpu.make_async_copy(d_hbm.at[:, cols], dx.at[g, pl.ds(0, ROWS)], lsem.at[5 + g]))
    weights = []
    for g in range(GROUPS):
        cols = pl.ds(g * STEP, STEP)
        weights.append(pltpu.make_async_copy(wk_hbm.at[:, cols], wk.at[g], lsem.at[9 + g]))
        weights.append(pltpu.make_async_copy(wv_hbm.at[:, cols], wv.at[g], lsem.at[13 + g]))
    for c in loads + weights:
        c.start()

    lane = lax.broadcasted_iota(jnp.int32, (1, 128), 1)
    row = jnp.zeros((1, 128), jnp.int32)
    owners, kin = [], []
    for r in range(REFS):
        entry = map_ref[r // 2, r % 2]
        owner = lax.div(entry, OWNED)
        row = jnp.where(lane == owner, lax.rem(entry, OWNED) + 1, row)
        owners.append(owner)
        kx = lax.rem(x - lax.div(owner, SIDE) + SIDE, SIDE)
        ky = lax.rem(y - lax.rem(owner, SIDE) + SIDE, SIDE)
        kin.append(kx * SIDE + ky)
    asked[...] = row
    tabv[0] = row
    con[...] = jnp.zeros_like(con)
    pl.semaphore_wait(barrier, PEERS + DEPTH - 1)

    def ask(k):
        return remote(asked, tabv.at[k], isend.at[k], irecv.at[k], seq=plane_peer(x, y, k))

    each(1, PEERS, lambda k: ask(k).start())
    each(1, PEERS, lambda k: ask(k).wait_recv())
    lc = pltpu.make_async_copy(tabv, tab, lsem.at[17])
    lc.start()
    enc_load.wait()
    lc.wait()

    def give_rows(k):
        return remote(send.at[k], slots.at[k, mine], ssend.at[k], srecv.at[k], seq=plane_peer(x, y, k))

    def share_rows(k):
        part = slots.at[k, mine]
        return remote(part, part, fsend.at[k], frecv.at[k], head=other)

    def start_rows(k):
        place = jnp.maximum(tab[opposite(k), 0, me] - 1, 0)
        send[k] = enc[place, mine, :]
        give_rows(k).start()

    each(1, PEERS, start_rows)
    for c in loads:
        c.wait()
    before = lax.rem(me + PEERS - 1, PEERS)
    halos = [
        remote(qx.at[:, pl.ds(0, RIM)], qx.at[:, pl.ds(ROWS, RIM)], halo_send.at[0], halo_recv.at[0], seq=before),
        remote(dx.at[:, pl.ds(0, RIM)], dx.at[:, pl.ds(ROWS, RIM)], halo_send.at[1], halo_recv.at[1], seq=before),
    ]
    for c in halos:
        c.start()
    slots[0] = enc[jnp.maximum(tab[0, 0, me] - 1, 0)]
    for c in weights:
        c.wait()

    def project(j):
        block = slots[pl.ds(2 * j, 2)].reshape(2 * NROWS, D_ENC)
        for g in range(GROUPS):
            keys[pl.ds(2 * j, 2), g] = nn(block, wk[g]).astype(BF).reshape(2, NROWS, STEP)
            vals[pl.ds(2 * j, 2), g] = nn(block, wv[g]).astype(BF).reshape(2, NROWS, STEP)
        enct[2 * j] = block[:NROWS].T
        enct[2 * j + 1] = block[NROWS:].T

    def arrive(k):
        give_rows(k).wait_recv()
        share_rows(k).start()

    arrive(1)

    def pair(j):
        @pl.when(j < PEERS // 2 - 1)
        def _():
            arrive(2 * j + 2)
            arrive(2 * j + 3)

        @pl.when(j > 0)
        def _():
            share_rows(2 * j).wait_recv()

        share_rows(2 * j + 1).wait_recv()
        project(j)

    each(0, PEERS // 2, pair)
    for c in halos:
        c.wait()
    for r in range(REFS):
        refs_t[:, pl.ds(r * NROWS, NROWS)] = enct[kin[r]]

    move = shift_matrix(ROWS, ROWS + RIM, RIM - 1)
    inside = lax.broadcasted_iota(jnp.int32, (ROWS, ROWS + RIM), 1) < jnp.where(me == PEERS - 1, ROWS, ROWS + RIM)
    move = jnp.where(inside, up(move), 0.0).astype(BF)
    col = lax.broadcasted_iota(jnp.int32, (SPAN, 2 * NROWS), 1)

    def first_a(g, k):
        xp = lax.rem(x + k, SIDE)
        return remote(dw.at[g, 0, xp], r1a.at[g, k - 1], send1a.at[g, k - 1], recv1a.at[g, k - 1], seq=xp * SIDE + y)

    def first_b(g, k):
        yp = lax.rem(y + k, SIDE)
        return remote(dw.at[g, 1, :, yp], r1b.at[g, k - 1], send1b.at[g, k - 1], recv1b.at[g, k - 1], seq=x * SIDE + yp)

    def group(g):
        qs = nn(move, qx[g]).astype(BF)
        do = nn(move, dx[g]).astype(BF)
        units = [(c, h) for c in range(REFS // 2) for h in range(STEP // HD)]

        def cut(a, c, h):
            return a[c * SPAN : (c + 1) * SPAN, h * HD : (h + 1) * HD]

        def both(a, c, h):
            return jnp.concatenate([a[kin[2 * c + n], g, :, pl.ds(h * HD, HD)] for n in range(2)], axis=0)

        k_u = [both(keys, c, h) for c, h in units]
        v_u = [both(vals, c, h) for c, h in units]
        q_u = [cut(qs, c, h) for c, h in units]
        d_u = [cut(do, c, h) for c, h in units]
        scores = [nt(q, k) * scale for q, k in zip(q_u, k_u)]
        dprobs = [nt(d, v) for d, v in zip(d_u, v_u)]
        probs_b, ds_b = [], []
        for (c, h), s, dp in zip(units, scores, dprobs):
            s = jnp.where(col < cnt_ref[0, c] * NROWS, s, -1e30)
            w = jnp.exp(s - jnp.max(s, axis=-1, keepdims=True))
            p = w / jnp.sum(w, axis=-1, keepdims=True)
            pb = p.astype(BF)
            delta = jnp.sum(up(pb) * dp, axis=-1, keepdims=True)
            probs_b.append(pb)
            ds_b.append((p * (dp - delta)).astype(BF))
        for (c, h), q, d, k, pb, ds in zip(units, q_u, d_u, k_u, probs_b, ds_b):
            at = (g, pl.ds(c * 2 * NROWS, 2 * NROWS), pl.ds(h * HD, HD))
            gs[g, pl.ds(c * SPAN, SPAN), pl.ds(h * HD, HD)] = (nn(ds, k) * scale).astype(BF)
            dk[at] = (tn(ds, q) * scale).astype(BF)
            dv[at] = tn(pb, d).astype(BF)
        dw[g, 0] = nn(refs_t[...], dk[g]).astype(BF).reshape(SIDE, SIDE, SHARE, STEP)
        dw[g, 1] = nn(refs_t[...], dv[g]).astype(BF).reshape(SIDE, SIDE, SHARE, STEP)
        for k in (2, 1, 3):
            first_a(g, k).start()
            first_b(g, k).start()
        more = nt(dk[g], wk[g]) + nt(dv[g], wv[g])
        con[...] += more.reshape(REFS, NROWS, D_ENC)

    each(0, GROUPS, group)

    swap = remote(con.at[:, theirs], hbuf, swap_sem.at[0], swap_sem.at[1], head=other)
    swap.start()
    after = lax.rem(me + 1, PEERS)
    halo = remote(gs.at[:, pl.ds(ROWS - RIM, RIM)], prev, prev_sem.at[0], prev_sem.at[1], seq=after)
    halo.start()
    swap.wait()
    for r in range(REFS):
        half[r] = (con[r, mine, :] + hbuf[r]).astype(BF)

    def ref_for(peer):
        found = jnp.int32(0)
        for r in range(REFS):
            found = jnp.where(owners[r] == peer, jnp.int32(r), found)
        return found

    each(1, PEERS, lambda k: give_rows(k).wait_send())

    def return_rows(k):
        return remote(send.at[k], recv.at[k], rsend.at[k], rrecv.at[k], seq=plane_peer(x, y, k))

    def start_return(k):
        send[k] = half[ref_for(plane_peer(x, y, k))]
        return_rows(k).start()

    each(1, PEERS, start_return)
    recv[0] = half[ref_for(me)]

    def second_a(g, k):
        yp = lax.rem(y + k, SIDE)
        return remote(s2a.at[g, yp], r2a.at[g, k - 1], send2a.at[g, k - 1], recv2a.at[g, k - 1], seq=x * SIDE + yp)

    def second_b(g, k):
        xp = lax.rem(x + k, SIDE)
        return remote(s2b.at[g, xp], r2b.at[g, k - 1], send2b.at[g, k - 1], recv2b.at[g, k - 1], seq=xp * SIDE + y)

    def sum_first(g):
        for k in (1, 2, 3):
            first_a(g, k).wait()
            first_b(g, k).wait()
        for j in range(SIDE):
            s2a[g, j] = (up(dw[g, 0, x, j]) + up(r1a[g, 0, j]) + up(r1a[g, 1, j]) + up(r1a[g, 2, j])).astype(BF)
            s2b[g, j] = (up(dw[g, 1, j, y]) + up(r1b[g, 0, j]) + up(r1b[g, 1, j]) + up(r1b[g, 2, j])).astype(BF)
        for k in (2, 1, 3):
            second_a(g, k).start()
            second_b(g, k).start()

    each(0, GROUPS, sum_first)

    halo.wait()
    old = jnp.where(me == 0, 0.0, 1.0)
    back_move = shift_matrix(ROWS, ROWS + RIM, 1)
    for g in range(GROUPS):
        ext = jnp.concatenate([(up(prev[g]) * old).astype(BF), gs[g]], axis=0)
        gqv[:, pl.ds(g * STEP, STEP)] = nn(back_move, ext).astype(BF)
    gq_out = pltpu.make_async_copy(gqv, gq_hbm, osem.at[0])
    gq_out.start()

    m = lax.broadcasted_iota(jnp.int32, (DEPTH * 8, SHARE), 0)
    e = lax.broadcasted_iota(jnp.int32, (DEPTH * 8, SHARE), 1)
    spread = jnp.logical_and(m // 8 * PIECE + m % 8 == e, m % 8 < PIECE).astype(F32).astype(BF)
    for g in range(GROUPS):
        for k in (1, 2, 3):
            second_a(g, k).wait()
            second_b(g, k).wait()
        own_a = up(dw[g, 0, x, y]) + up(r1a[g, 0, y]) + up(r1a[g, 1, y]) + up(r1a[g, 2, y])
        own_b = up(dw[g, 1, x, y]) + up(r1b[g, 0, x]) + up(r1b[g, 1, x]) + up(r1b[g, 2, x])
        t_a = (own_a + up(r2a[g, 0]) + up(r2a[g, 1]) + up(r2a[g, 2])).astype(BF)
        t_b = (own_b + up(r2b[g, 0]) + up(r2b[g, 1]) + up(r2b[g, 2])).astype(BF)
        cols = pl.ds(g * STEP, STEP)
        s3[:, 0, :, cols] = nn(spread, t_a).astype(BF).reshape(DEPTH, 8, STEP)
        s3[:, 1, :, cols] = nn(spread, t_b).astype(BF).reshape(DEPTH, 8, STEP)

    def third(k):
        zp = lax.rem(level + k, DEPTH)
        return remote(s3.at[zp], r3.at[k], send3.at[k], recv3.at[k], dp=zp)

    each(1, DEPTH, lambda k: third(k).start())

    each(1, PEERS, lambda k: return_rows(k).wait_recv())
    place = lax.broadcasted_iota(jnp.int32, (OWNED * HALF, 2 * HALF), 0)
    slot = lax.broadcasted_iota(jnp.int32, (OWNED * HALF, 2 * HALF), 1)
    pick = []
    for t in range(PEERS // 2):
        lo = (tab[2 * t, 0, me] - 1) * HALF
        hi = (tab[2 * t + 1, 0, me] - 1) * HALF
        target = jnp.where(slot < HALF, slot + lo, slot - HALF + hi)
        live = jnp.where(slot < HALF, lo, hi) >= 0
        pick.append(jnp.logical_and(place == target, live).astype(F32).astype(BF))
    total = nn(jnp.concatenate(pick, axis=1), recv[...].reshape(PEERS * HALF, D_ENC))
    ohalf[...] = total.astype(BF).reshape(OWNED, HALF, D_ENC)
    back = remote(ohalf, ge_hbm.at[:, mine], back_sem.at[0], back_sem.at[1], head=other)
    back.start()
    ge_out = pltpu.make_async_copy(ohalf, ge_hbm.at[:, mine], osem.at[1])
    ge_out.start()

    each(1, DEPTH, lambda k: third(k).wait())
    final = up(s3[level])
    for k in range(1, DEPTH):
        final = final + up(r3[k])
    gw_ref[:, 0, :] = final[0, :PIECE]
    gw_ref[:, 1, :] = final[1, :PIECE]

    each(1, PEERS, lambda k: ask(k).wait_send())
    each(1, PEERS, lambda k: share_rows(k).wait_send())
    each(1, PEERS, lambda k: return_rows(k).wait_send())
    gq_out.wait()
    ge_out.wait()
    back.wait()


def body(queries, out_grad, encodings, owner_map, nbr_count, key_weight, value_weight):
    vm = pl.BlockSpec(memory_space=pltpu.VMEM)
    sm = pl.BlockSpec(memory_space=pltpu.SMEM)
    hbm = pl.BlockSpec(memory_space=pl.ANY)
    dma = pltpu.SemaphoreType.DMA

    def bf(*shape):
        return pltpu.VMEM(shape, BF)

    gq, ge, gw = pl.pallas_call(
        kernel,
        out_shape=(
            jax.ShapeDtypeStruct((ROWS, FEAT), BF),
            jax.ShapeDtypeStruct((OWNED, NROWS, D_ENC), BF),
            jax.ShapeDtypeStruct((PIECE, 2, FEAT), F32),
        ),
        in_specs=[sm, sm, hbm, hbm, hbm, hbm, hbm],
        out_specs=(hbm, hbm, vm),
        scratch_shapes=[
            bf(OWNED, NROWS, D_ENC),
            bf(GROUPS, D_ENC, STEP),
            bf(GROUPS, D_ENC, STEP),
            bf(GROUPS, ROWS + RIM, STEP),
            bf(GROUPS, ROWS + RIM, STEP),
            pltpu.VMEM((1, 128), jnp.int32),
            pltpu.VMEM((PEERS, 1, 128), jnp.int32),
            pltpu.SMEM((PEERS, 1, 128), jnp.int32),
            bf(PEERS, HALF, D_ENC),
            bf(PEERS, NROWS, D_ENC),
            bf(PEERS, GROUPS, NROWS, STEP),
            bf(PEERS, GROUPS, NROWS, STEP),
            bf(PEERS, D_ENC, NROWS),
            bf(D_ENC, REFS * NROWS),
            bf(GROUPS, REFS * NROWS, STEP),
            bf(GROUPS, REFS * NROWS, STEP),
            pltpu.VMEM((REFS, NROWS, D_ENC), F32),
            pltpu.VMEM((REFS, HALF, D_ENC), F32),
            bf(REFS, HALF, D_ENC),
            bf(PEERS, HALF, D_ENC),
            bf(OWNED, HALF, D_ENC),
            bf(GROUPS, ROWS, STEP),
            bf(GROUPS, RIM, STEP),
            bf(ROWS, FEAT),
            bf(GROUPS, 2, SIDE, SIDE, SHARE, STEP),
            bf(GROUPS, SIDE - 1, SIDE, SHARE, STEP),
            bf(GROUPS, SIDE - 1, SIDE, SHARE, STEP),
            bf(GROUPS, SIDE, SHARE, STEP),
            bf(GROUPS, SIDE, SHARE, STEP),
            bf(GROUPS, SIDE - 1, SHARE, STEP),
            bf(GROUPS, SIDE - 1, SHARE, STEP),
            bf(DEPTH, 2, 8, FEAT),
            bf(DEPTH, 2, 8, FEAT),
            dma((18,)), dma((2,)),
            dma((PEERS,)), dma((PEERS,)), dma((PEERS,)), dma((PEERS,)), dma((PEERS,)), dma((PEERS,)),
            dma((2,)), dma((2,)), dma((2,)),
            dma((PEERS,)), dma((PEERS,)), dma((2,)), dma((2,)),
            dma((GROUPS, 3)), dma((GROUPS, 3)), dma((GROUPS, 3)), dma((GROUPS, 3)),
            dma((GROUPS, 3)), dma((GROUPS, 3)), dma((GROUPS, 3)), dma((GROUPS, 3)),
            dma((DEPTH,)), dma((DEPTH,)),
        ],
        compiler_params=pltpu.CompilerParams(
            collective_id=0, has_side_effects=True, vmem_limit_bytes=VMEM_LIMIT
        ),
        name="spans",
    )(
        owner_map[0], nbr_count, encodings.reshape(OWNED, NROWS, D_ENC),
        queries[0], out_grad[0], key_weight, value_weight,
    )
    return gq[None], ge.reshape(1, OWNED * NROWS, D_ENC), gw


def solution(mesh):
    return jax.shard_map(
        body,
        mesh=mesh,
        in_specs=(
            P("dp", "seq", "head"),
            P("dp", "seq", "head"),
            P("dp", "seq", None),
            P("dp", "seq", None),
            P("dp", "seq"),
            P(None, "head"),
            P(None, "head"),
        ),
        out_specs=(P("dp", "seq", "head"), P("dp", "seq", None), P(("seq", "dp"), None, "head")),
        check_vma=False,
    )
```

```python
import functools
import math

import jax
import jax.numpy as jnp
from jax import lax
from jax.experimental import pallas as pl
from jax.experimental.pallas import tpu as pltpu
from jax.sharding import PartitionSpec as P

MESH = pl.DeviceIdType.MESH
HD = 128
SPAN = 64
NROWS = 128
REFS = 8
SIDE = 4
PEERS = SIDE * SIDE
DEPTH = 8
HALF = NROWS // 2
OWNED = 8
D_ENC = 896
FEAT = 1024
ROWS = 256
RIM = 64
STEP = 256
GROUPS = FEAT // STEP
SHARE = D_ENC // PEERS
PIECE = SHARE // DEPTH
VMEM_LIMIT = 58 << 20
BF = jnp.bfloat16
F32 = jnp.float32


def ring(step):
    return min(step, SIDE - step)


STEPS = sorted(
    [(dx, dy) for dx in range(SIDE) for dy in range(SIDE)],
    key=lambda s: -(ring(s[0]) + ring(s[1])) if s != (0, 0) else -9,
)


def plane_place():
    me = lax.axis_index("seq")
    return me, lax.div(me, SIDE), lax.rem(me, SIDE)


def plane_peer(x, y, i):
    dx, dy = STEPS[i]
    return lax.rem(x + dx, SIDE) * SIDE + lax.rem(y + dy, SIDE)


def opposite(i):
    dx, dy = STEPS[i]
    return STEPS.index((-dx % SIDE, -dy % SIDE))


def each(start, stop, step):
    def one(k, carry):
        step(k)
        return carry

    lax.fori_loop(start, stop, one, 0)


def up(a):
    return a.astype(F32)


def remote(src, dst, send_sem, recv_sem, **where):
    return pltpu.make_async_remote_copy(
        src_ref=src,
        dst_ref=dst,
        send_sem=send_sem,
        recv_sem=recv_sem,
        device_id=where,
        device_id_type=MESH,
    )


def greet(barrier, **where):
    pl.semaphore_signal(barrier, inc=1, device_id=where, device_id_type=MESH)


def nt(a, b):
    return lax.dot_general(a, b, (((1,), (1,)), ((), ())), preferred_element_type=F32)


def tn(a, b):
    return lax.dot_general(a, b, (((0,), (0,)), ((), ())), preferred_element_type=F32)


def nn(a, b):
    return jnp.dot(a, b, preferred_element_type=F32)


def shift_matrix(rows, columns, by):
    i = lax.broadcasted_iota(jnp.int32, (rows, columns), 0)
    e = lax.broadcasted_iota(jnp.int32, (rows, columns), 1)
    return (e == i + by).astype(F32).astype(BF)


def kernel(
    map_ref, cnt_ref, enc_hbm, q_hbm, d_hbm, wk_hbm, wv_hbm,
    gq_hbm, ge_hbm, gw_ref,
    enc, w, qx, dx, asked, tabv, tab, send, slots, kv, enct, refs_t,
    dkv, con, hbuf, half, recv, ohalf, gs, prev, gqv, dw, r1a, r1b, s2a, s2b, r2a, r2b, s3, r3,
    lsem, osem, isend, irecv, ssend, srecv, fsend, frecv, halo_send, halo_recv,
    swap_sem, rsend, rrecv, back_sem, prev_sem,
    send1a, recv1a, send1b, recv1b, send2a, recv2a, send2b, recv2b, send3, recv3,
):
    me, x, y = plane_place()
    core = lax.axis_index("head")
    level = lax.axis_index("dp")
    other = 1 - core
    scale = 1.0 / math.sqrt(HD)
    mine = pl.ds(pl.multiple_of(core * HALF, HALF), HALF)
    theirs = pl.ds(pl.multiple_of(other * HALF, HALF), HALF)
    before = lax.rem(me + PEERS - 1, PEERS)
    after = lax.rem(me + 1, PEERS)

    barrier = pltpu.get_barrier_semaphore()
    for i in range(1, PEERS):
        greet(barrier, seq=plane_peer(x, y, i))
    greet(barrier, head=other)
    each(1, DEPTH, lambda k: greet(barrier, dp=lax.rem(level + k, DEPTH)))

    enc_load = pltpu.make_async_copy(enc_hbm, enc, lsem.at[0])
    loads = [
        pltpu.make_async_copy(q_hbm, qx.at[pl.ds(0, ROWS)], lsem.at[1]),
        pltpu.make_async_copy(d_hbm, dx.at[pl.ds(0, ROWS)], lsem.at[2]),
    ]
    weights = [
        pltpu.make_async_copy(wk_hbm, w.at[:, pl.ds(0, FEAT)], lsem.at[3]),
        pltpu.make_async_copy(wv_hbm, w.at[:, pl.ds(FEAT, FEAT)], lsem.at[4]),
    ]
    for c in [enc_load] + weights + loads:
        c.start()

    lane = lax.broadcasted_iota(jnp.int32, (1, 128), 1)
    row = jnp.zeros((1, 128), jnp.int32)
    owners, kin = [], []
    for r in range(REFS):
        entry = map_ref[0, r // 2, r % 2]
        owner = lax.div(entry, OWNED)
        row = jnp.where(lane == owner, lax.rem(entry, OWNED) + 1, row)
        owners.append(owner)
        kx = lax.rem(x - lax.div(owner, SIDE) + SIDE, SIDE)
        ky = lax.rem(y - lax.rem(owner, SIDE) + SIDE, SIDE)
        found = jnp.int32(0)
        for i in range(1, PEERS):
            found = jnp.where(kx * SIDE + ky == STEPS[i][0] * SIDE + STEPS[i][1], jnp.int32(i), found)
        kin.append(found)
    asked[...] = row
    tabv[0] = row
    pl.semaphore_wait(barrier, PEERS + DEPTH - 1)

    def ask(i, peer):
        return remote(asked, tabv.at[i], isend.at[i], irecv.at[i], seq=peer)

    for i in range(1, PEERS):
        ask(i, plane_peer(x, y, i)).start()
    halos = [
        remote(q_hbm.at[pl.ds(0, RIM)], qx.at[pl.ds(ROWS, RIM)], halo_send.at[0], halo_recv.at[0], seq=before),
        remote(d_hbm.at[pl.ds(0, RIM)], dx.at[pl.ds(ROWS, RIM)], halo_send.at[1], halo_recv.at[1], seq=before),
    ]
    for c in halos:
        c.start()
    each(1, PEERS, lambda i: ask(i, after).wait_recv())
    lc = pltpu.make_async_copy(tabv, tab, lsem.at[5])
    lc.start()
    enc_load.wait()
    lc.wait()

    def give_rows(i, peer):
        return remote(send.at[i], slots.at[i, mine], ssend.at[i], srecv.at[i], seq=peer)

    def share_rows(i):
        part = slots.at[i, mine]
        return remote(part, part, fsend.at[i], frecv.at[i], head=other)

    for i in range(1, PEERS):
        place = jnp.maximum(tab[opposite(i), 0, me] - 1, 0)
        send[i] = enc[place, mine, :]
        give_rows(i, plane_peer(x, y, i)).start()
    slots[0] = enc[jnp.maximum(tab[0, 0, me] - 1, 0)]
    for c in weights:
        c.wait()

    def project(j):
        block = slots[pl.ds(2 * j, 2)].reshape(2 * NROWS, D_ENC)
        for g in range(2 * GROUPS):
            cols = pl.ds(g * STEP, STEP)
            kv[pl.ds(2 * j, 2), :, cols] = nn(block, w[:, cols]).astype(BF).reshape(2, NROWS, STEP)
        enct[2 * j] = block[:NROWS].T
        enct[2 * j + 1] = block[NROWS:].T

    def arrive(i):
        give_rows(i, after).wait_recv()
        share_rows(i).start()

    arrive(1)

    def pair(j):
        @pl.when(j < PEERS // 2 - 1)
        def _():
            arrive(2 * j + 2)
            arrive(2 * j + 3)

        @pl.when(j > 0)
        def _():
            share_rows(2 * j).wait_recv()

        share_rows(2 * j + 1).wait_recv()
        project(j)

    each(0, PEERS // 2, pair)
    for c in loads:
        c.wait()
    for c in halos:
        c.wait()
    for r in range(REFS):
        refs_t[:, pl.ds(r * NROWS, NROWS)] = enct[kin[r]]

    move = shift_matrix(ROWS, ROWS + RIM, RIM - 1)
    inside = lax.broadcasted_iota(jnp.int32, (ROWS, ROWS + RIM), 1) < jnp.where(me == PEERS - 1, ROWS, ROWS + RIM)
    move = jnp.where(inside, up(move), 0.0).astype(BF)
    col = lax.broadcasted_iota(jnp.int32, (SPAN, 2 * NROWS), 1)

    def first_a(g, k):
        xp = lax.rem(x + k, SIDE)
        return remote(dw.at[g, 0, xp], r1a.at[g, k - 1], send1a.at[g, k - 1], recv1a.at[g, k - 1], seq=xp * SIDE + y)

    def first_b(g, k):
        yp = lax.rem(y + k, SIDE)
        return remote(dw.at[g, 1, :, yp], r1b.at[g, k - 1], send1b.at[g, k - 1], recv1b.at[g, k - 1], seq=x * SIDE + yp)

    def second_a(p, k):
        yp = lax.rem(y + k, SIDE)
        return remote(s2a.at[p, :, yp], r2a.at[p, k - 1], send2a.at[p, k - 1], recv2a.at[p, k - 1], seq=x * SIDE + yp)

    def second_b(p, k):
        xp = lax.rem(x + k, SIDE)
        return remote(s2b.at[p, :, xp], r2b.at[p, k - 1], send2b.at[p, k - 1], recv2b.at[p, k - 1], seq=xp * SIDE + y)

    def sum_first(g):
        for k in (1, 2, 3):
            first_a(g, k).wait()
            first_b(g, k).wait()
        p, n = lax.div(g, 2), lax.rem(g, 2)
        for j in range(SIDE):
            s2a[p, n, j] = (up(dw[g, 0, x, j]) + up(r1a[g, 0, j]) + up(r1a[g, 1, j]) + up(r1a[g, 2, j])).astype(BF)
            s2b[p, n, j] = (up(dw[g, 1, j, y]) + up(r1b[g, 0, j]) + up(r1b[g, 1, j]) + up(r1b[g, 2, j])).astype(BF)

    def start_second(p):
        for k in (2, 1, 3):
            second_a(p, k).start()
            second_b(p, k).start()

    def group(g):
        cols = pl.ds(pl.multiple_of(g * STEP, STEP), STEP)
        cols_v = pl.ds(pl.multiple_of(g * STEP + FEAT, STEP), STEP)
        qs = nn(move, qx[:, cols]).astype(BF)
        do = nn(move, dx[:, cols]).astype(BF)
        units = [(c, h) for c in range(REFS // 2) for h in range(STEP // HD)]

        def cut(a, c, h):
            return a[c * SPAN : (c + 1) * SPAN, h * HD : (h + 1) * HD]

        def head(h, base=0):
            return pl.ds(pl.multiple_of(g * STEP + h * HD + base, HD), HD)

        def both(c, h, base):
            return jnp.concatenate([kv[kin[2 * c + n], :, head(h, base)] for n in range(2)], axis=0)

        k_u = [both(c, h, 0) for c, h in units]
        v_u = [both(c, h, FEAT) for c, h in units]
        q_u = [cut(qs, c, h) for c, h in units]
        d_u = [cut(do, c, h) for c, h in units]
        scores = [nt(q, k) * scale for q, k in zip(q_u, k_u)]
        dprobs = [nt(d, v) for d, v in zip(d_u, v_u)]
        probs_b, ds_b = [], []
        for (c, h), s, dp in zip(units, scores, dprobs):
            s = jnp.where(col < cnt_ref[0, c] * NROWS, s, -1e30)
            e = jnp.exp(s - jnp.max(s, axis=-1, keepdims=True))
            p = e / jnp.sum(e, axis=-1, keepdims=True)
            pb = p.astype(BF)
            delta = jnp.sum(up(pb) * dp, axis=-1, keepdims=True)
            probs_b.append(pb)
            ds_b.append((p * (dp - delta)).astype(BF))
        for (c, h), q, d, k, pb, ds in zip(units, q_u, d_u, k_u, probs_b, ds_b):
            two = pl.ds(2 * c, 2)
            gs[pl.ds(c * SPAN, SPAN), head(h)] = (nn(ds, k) * scale).astype(BF)
            dkv[two, :, head(h)] = (tn(ds, q) * scale).astype(BF).reshape(2, NROWS, HD)
            dkv[two, :, head(h, FEAT)] = tn(pb, d).astype(BF).reshape(2, NROWS, HD)
        dk = dkv[:, :, cols].reshape(REFS * NROWS, STEP)
        dv = dkv[:, :, cols_v].reshape(REFS * NROWS, STEP)
        dw[g, 0] = nn(refs_t[...], dk).astype(BF).reshape(SIDE, SIDE, SHARE, STEP)
        dw[g, 1] = nn(refs_t[...], dv).astype(BF).reshape(SIDE, SIDE, SHARE, STEP)
        for k in (2, 1, 3):
            first_a(g, k).start()
            first_b(g, k).start()

        @pl.when(g >= 2)
        def _():
            sum_first(g - 2)

    each(0, GROUPS, group)
    start_second(0)

    con[...] = nt(dkv[:, theirs, :].reshape(REFS * HALF, 2 * FEAT), w[...]).reshape(REFS, HALF, D_ENC)
    swap = remote(con, hbuf, swap_sem.at[0], swap_sem.at[1], head=other)
    swap.start()
    own = nt(dkv[:, mine, :].reshape(REFS * HALF, 2 * FEAT), w[...]).reshape(REFS, HALF, D_ENC)
    swap.wait()
    half[...] = (own + hbuf[...]).astype(BF)

    def ref_for(peer):
        found = jnp.int32(0)
        for r in range(REFS):
            found = jnp.where(owners[r] == peer, jnp.int32(r), found)
        return found

    each(1, PEERS, lambda i: give_rows(i, after).wait_send())

    def return_rows(i, peer):
        return remote(send.at[i], recv.at[i], rsend.at[i], rrecv.at[i], seq=peer)

    for i in range(1, PEERS):
        peer = plane_peer(x, y, i)
        send[i] = half[ref_for(peer)]
        return_rows(i, peer).start()
    halo = remote(gs.at[pl.ds(ROWS - RIM, RIM)], prev, prev_sem.at[0], prev_sem.at[1], seq=after)
    halo.start()
    recv[0] = half[ref_for(me)]
    sum_first(2)
    sum_first(3)
    start_second(1)

    halo.wait()
    old = jnp.where(me == 0, 0.0, 1.0)
    ext = jnp.concatenate([(up(prev[...]) * old).astype(BF), gs[...]], axis=0)
    gqv[...] = nn(shift_matrix(ROWS, ROWS + RIM, 1), ext).astype(BF)
    gq_out = pltpu.make_async_copy(gqv, gq_hbm, osem.at[0])
    gq_out.start()

    m = lax.broadcasted_iota(jnp.int32, (DEPTH * 8, SHARE), 0)
    e = lax.broadcasted_iota(jnp.int32, (DEPTH * 8, SHARE), 1)
    spread = jnp.logical_and(m // 8 * PIECE + m % 8 == e, m % 8 < PIECE).astype(F32).astype(BF)
    for p in range(GROUPS // 2):
        for k in (1, 2, 3):
            second_a(p, k).wait()
            second_b(p, k).wait()
        for n in range(2):
            g = 2 * p + n
            own_a = up(dw[g, 0, x, y]) + up(r1a[g, 0, y]) + up(r1a[g, 1, y]) + up(r1a[g, 2, y])
            own_b = up(dw[g, 1, x, y]) + up(r1b[g, 0, x]) + up(r1b[g, 1, x]) + up(r1b[g, 2, x])
            t_a = (own_a + up(r2a[p, 0, n]) + up(r2a[p, 1, n]) + up(r2a[p, 2, n])).astype(BF)
            t_b = (own_b + up(r2b[p, 0, n]) + up(r2b[p, 1, n]) + up(r2b[p, 2, n])).astype(BF)
            cols = pl.ds(g * STEP, STEP)
            s3[:, 0, :, cols] = nn(spread, t_a).astype(BF).reshape(DEPTH, 8, STEP)
            s3[:, 1, :, cols] = nn(spread, t_b).astype(BF).reshape(DEPTH, 8, STEP)

    def third(k):
        zp = lax.rem(level + k, DEPTH)
        return remote(s3.at[zp], r3.at[k], send3.at[k], recv3.at[k], dp=zp)

    for k in (4, 3, 5, 2, 6, 1, 7):
        third(k).start()

    place = lax.broadcasted_iota(jnp.int32, (OWNED * HALF, 2 * HALF), 0)
    slot = lax.broadcasted_iota(jnp.int32, (OWNED * HALF, 2 * HALF), 1)
    pick = []
    for t in range(PEERS // 2):
        lo = (tab[2 * t, 0, me] - 1) * HALF
        hi = (tab[2 * t + 1, 0, me] - 1) * HALF
        target = jnp.where(slot < HALF, slot + lo, slot - HALF + hi)
        live = jnp.where(slot < HALF, lo, hi) >= 0
        pick.append(jnp.logical_and(place == target, live).astype(F32).astype(BF))
    pick = jnp.concatenate(pick, axis=1)
    each(1, PEERS, lambda i: return_rows(i, after).wait_recv())
    total = nn(pick, recv[...].reshape(PEERS * HALF, D_ENC))
    ohalf[...] = total.astype(BF).reshape(OWNED, HALF, D_ENC)
    back = remote(ohalf, ge_hbm.at[:, mine], back_sem.at[0], back_sem.at[1], head=other)
    back.start()
    ge_out = pltpu.make_async_copy(ohalf, ge_hbm.at[:, mine], osem.at[1])
    ge_out.start()

    each(1, DEPTH, lambda k: third(k).wait())
    final = up(s3[level])
    for k in range(1, DEPTH):
        final = final + up(r3[k])
    gw_ref[:, 0, :] = final[0, :PIECE]
    gw_ref[:, 1, :] = final[1, :PIECE]

    each(1, PEERS, lambda i: ask(i, after).wait_send())
    each(1, PEERS, lambda i: share_rows(i).wait_send())
    each(1, PEERS, lambda i: return_rows(i, after).wait_send())
    gq_out.wait()
    ge_out.wait()
    back.wait()


def finish_kernel(gq, ge, gw, gq_out, ge_out, gw_out, sems):
    copies = [pltpu.make_async_copy(gw, gw_out, sems.at[0])]
    for n in range(4):
        two = pl.ds(2 * n, 2)
        copies.append(pltpu.make_async_copy(ge.at[two], ge_out.at[two], sems.at[1 + n]))
    for n in range(2):
        rows = pl.ds(n * ROWS // 2, ROWS // 2)
        copies.append(pltpu.make_async_copy(gq.at[rows], gq_out.at[rows], sems.at[5 + n]))
    for c in copies:
        c.start()
    for c in copies:
        c.wait()


def body(queries, out_grad, encodings, owner_map, nbr_count, key_weight, value_weight):
    vm = pl.BlockSpec(memory_space=pltpu.VMEM)
    sm = pl.BlockSpec(memory_space=pltpu.SMEM)
    hbm = pl.BlockSpec(memory_space=pl.ANY)
    dma = pltpu.SemaphoreType.DMA

    def bf(*shape):
        return pltpu.VMEM(shape, BF)

    gq, ge, gw = pl.pallas_call(
        kernel,
        out_shape=(
            jax.ShapeDtypeStruct((ROWS, FEAT), BF),
            jax.ShapeDtypeStruct((OWNED, NROWS, D_ENC), BF),
            jax.ShapeDtypeStruct((PIECE, 2, FEAT), F32),
        ),
        in_specs=[sm, sm, hbm, hbm, hbm, hbm, hbm],
        out_specs=(hbm, hbm, vm),
        scratch_shapes=[
            bf(OWNED, NROWS, D_ENC),
            bf(D_ENC, 2 * FEAT),
            bf(ROWS + RIM, FEAT),
            bf(ROWS + RIM, FEAT),
            pltpu.VMEM((1, 128), jnp.int32),
            pltpu.VMEM((PEERS, 1, 128), jnp.int32),
            pltpu.SMEM((PEERS, 1, 128), jnp.int32),
            bf(PEERS, HALF, D_ENC),
            bf(PEERS, NROWS, D_ENC),
            bf(PEERS, NROWS, 2 * FEAT),
            bf(PEERS, D_ENC, NROWS),
            bf(D_ENC, REFS * NROWS),
            bf(REFS, NROWS, 2 * FEAT),
            pltpu.VMEM((REFS, HALF, D_ENC), F32),
            pltpu.VMEM((REFS, HALF, D_ENC), F32),
            bf(REFS, HALF, D_ENC),
            bf(PEERS, HALF, D_ENC),
            bf(OWNED, HALF, D_ENC),
            bf(ROWS, FEAT),
            bf(RIM, FEAT),
            bf(ROWS, FEAT),
            bf(GROUPS, 2, SIDE, SIDE, SHARE, STEP),
            bf(GROUPS, SIDE - 1, SIDE, SHARE, STEP),
            bf(GROUPS, SIDE - 1, SIDE, SHARE, STEP),
            bf(GROUPS // 2, 2, SIDE, SHARE, STEP),
            bf(GROUPS // 2, 2, SIDE, SHARE, STEP),
            bf(GROUPS // 2, SIDE - 1, 2, SHARE, STEP),
            bf(GROUPS // 2, SIDE - 1, 2, SHARE, STEP),
            bf(DEPTH, 2, 8, FEAT),
            bf(DEPTH, 2, 8, FEAT),
            dma((6,)), dma((2,)),
            dma((PEERS,)), dma((PEERS,)), dma((PEERS,)), dma((PEERS,)), dma((PEERS,)), dma((PEERS,)),
            dma((2,)), dma((2,)), dma((2,)),
            dma((PEERS,)), dma((PEERS,)), dma((2,)), dma((2,)),
            dma((GROUPS, 3)), dma((GROUPS, 3)), dma((GROUPS, 3)), dma((GROUPS, 3)),
            dma((2, 3)), dma((2, 3)), dma((2, 3)), dma((2, 3)),
            dma((DEPTH,)), dma((DEPTH,)),
        ],
        compiler_params=pltpu.CompilerParams(
            collective_id=0, has_side_effects=True, vmem_limit_bytes=VMEM_LIMIT
        ),
        name="spans",
    )(
        owner_map, nbr_count, encodings.reshape(OWNED, NROWS, D_ENC),
        queries[0], out_grad[0], key_weight, value_weight,
    )
    gq, ge, gw = pl.pallas_call(
        finish_kernel,
        out_shape=tuple(jax.ShapeDtypeStruct(a.shape, a.dtype) for a in (gq, ge, gw)),
        in_specs=[hbm] * 3,
        out_specs=(hbm,) * 3,
        scratch_shapes=[dma((7,))],
        name="finish",
    )(gq, ge, gw)
    return gq[None], ge.reshape(1, OWNED * NROWS, D_ENC), gw


def solution(mesh):
    return jax.shard_map(
        body,
        mesh=mesh,
        in_specs=(
            P("dp", "seq", "head"),
            P("dp", "seq", "head"),
            P("dp", "seq", None),
            P("dp", "seq", None),
            P("dp", "seq"),
            P(None, "head"),
            P(None, "head"),
        ),
        out_specs=(P("dp", "seq", "head"), P("dp", "seq", None), P(("seq", "dp"), None, "head")),
        check_vma=False,
    )
```

```python
import functools
import math

import jax
import jax.numpy as jnp
from jax import lax
from jax.experimental import pallas as pl
from jax.experimental.pallas import tpu as pltpu
from jax.sharding import PartitionSpec as P

MESH = pl.DeviceIdType.MESH
HD = 128
SPAN = 64
NROWS = 128
REFS = 8
SIDE = 4
PEERS = SIDE * SIDE
DEPTH = 8
HALF = NROWS // 2
OWNED = 8
D_ENC = 896
FEAT = 1024
ROWS = 256
RIM = 64
STEP = 256
GROUPS = FEAT // STEP
SHARE = D_ENC // PEERS
PIECE = SHARE // DEPTH
VMEM_LIMIT = 58 << 20
BF = jnp.bfloat16
F32 = jnp.float32


def ring(step):
    return min(step, SIDE - step)


STEPS = sorted(
    [(dx, dy) for dx in range(SIDE) for dy in range(SIDE)],
    key=lambda s: -(ring(s[0]) + ring(s[1])) if s != (0, 0) else -9,
)


def plane_place():
    me = lax.axis_index("seq")
    return me, lax.div(me, SIDE), lax.rem(me, SIDE)


def plane_peer(x, y, i):
    dx, dy = STEPS[i]
    return lax.rem(x + dx, SIDE) * SIDE + lax.rem(y + dy, SIDE)


def opposite(i):
    dx, dy = STEPS[i]
    return STEPS.index((-dx % SIDE, -dy % SIDE))


def each(start, stop, step):
    def one(k, carry):
        step(k)
        return carry

    lax.fori_loop(start, stop, one, 0)


def up(a):
    return a.astype(F32)


def remote(src, dst, send_sem, recv_sem, **where):
    return pltpu.make_async_remote_copy(
        src_ref=src,
        dst_ref=dst,
        send_sem=send_sem,
        recv_sem=recv_sem,
        device_id=where,
        device_id_type=MESH,
    )


def greet(barrier, **where):
    pl.semaphore_signal(barrier, inc=1, device_id=where, device_id_type=MESH)


def nt(a, b):
    return lax.dot_general(a, b, (((1,), (1,)), ((), ())), preferred_element_type=F32)


def tn(a, b):
    return lax.dot_general(a, b, (((0,), (0,)), ((), ())), preferred_element_type=F32)


def nn(a, b):
    return jnp.dot(a, b, preferred_element_type=F32)


def shift_matrix(rows, columns, by):
    i = lax.broadcasted_iota(jnp.int32, (rows, columns), 0)
    e = lax.broadcasted_iota(jnp.int32, (rows, columns), 1)
    return (e == i + by).astype(F32).astype(BF)


def kernel(
    map_ref, cnt_ref, enc_hbm, q_hbm, d_hbm, wk_hbm, wv_hbm,
    gq_hbm, ge_hbm, gw_ref,
    enc, w, qx, dx, asked, tabv, tab, send, slots, kv, enct, refs_t,
    dkv, con, hbuf, half, recv, ohalf, gs, prev, gqv, dw, r1a, r1b, s2a, s2b, r2a, r2b, s3, r3, zs, zr, zt, zu,
    lsem, osem, isend, irecv, ssend, srecv, fsend, frecv, halo_send, halo_recv,
    swap_sem, rsend, rrecv, back_sem, prev_sem,
    send1a, recv1a, send1b, recv1b, send2a, recv2a, send2b, recv2b, send3, recv3, zsend, zrecv, tsend, trecv,
):
    me, x, y = plane_place()
    core = lax.axis_index("head")
    level = lax.axis_index("dp")
    other = 1 - core
    scale = 1.0 / math.sqrt(HD)
    mine = pl.ds(pl.multiple_of(core * HALF, HALF), HALF)
    theirs = pl.ds(pl.multiple_of(other * HALF, HALF), HALF)
    before = lax.rem(me + PEERS - 1, PEERS)
    after = lax.rem(me + 1, PEERS)

    barrier = pltpu.get_barrier_semaphore()
    for i in range(1, PEERS):
        greet(barrier, seq=plane_peer(x, y, i))
    greet(barrier, head=other)
    each(1, DEPTH, lambda k: greet(barrier, dp=lax.rem(level + k, DEPTH)))

    enc_load = pltpu.make_async_copy(enc_hbm, enc, lsem.at[0])
    loads = [
        pltpu.make_async_copy(q_hbm, qx.at[pl.ds(0, ROWS)], lsem.at[1]),
        pltpu.make_async_copy(d_hbm, dx.at[pl.ds(0, ROWS)], lsem.at[2]),
    ]
    weights = [
        pltpu.make_async_copy(wk_hbm, w.at[:, pl.ds(0, FEAT)], lsem.at[3]),
        pltpu.make_async_copy(wv_hbm, w.at[:, pl.ds(FEAT, FEAT)], lsem.at[4]),
    ]
    for c in [enc_load] + weights + loads:
        c.start()

    lane = lax.broadcasted_iota(jnp.int32, (1, 128), 1)
    row = jnp.zeros((1, 128), jnp.int32)
    owners, kin = [], []
    for r in range(REFS):
        entry = map_ref[0, r % 2, r // 2]
        owner = lax.div(entry, OWNED)
        row = jnp.where(lane == owner, lax.rem(entry, OWNED) + 1, row)
        owners.append(owner)
        kx = lax.rem(x - lax.div(owner, SIDE) + SIDE, SIDE)
        ky = lax.rem(y - lax.rem(owner, SIDE) + SIDE, SIDE)
        found = jnp.int32(0)
        for i in range(1, PEERS):
            found = jnp.where(kx * SIDE + ky == STEPS[i][0] * SIDE + STEPS[i][1], jnp.int32(i), found)
        kin.append(found)
    asked[...] = row
    tabv[0] = row
    pl.semaphore_wait(barrier, PEERS + DEPTH - 1)

    def ask(i, peer):
        return remote(asked, tabv.at[i], isend.at[i], irecv.at[i], seq=peer)

    for i in range(1, PEERS):
        ask(i, plane_peer(x, y, i)).start()
    halos = [
        remote(q_hbm.at[pl.ds(0, RIM)], qx.at[pl.ds(ROWS, RIM)], halo_send.at[0], halo_recv.at[0], seq=before),
        remote(d_hbm.at[pl.ds(0, RIM)], dx.at[pl.ds(ROWS, RIM)], halo_send.at[1], halo_recv.at[1], seq=before),
    ]
    for c in halos:
        c.start()
    each(1, PEERS, lambda i: ask(i, after).wait_recv())
    lc = pltpu.make_async_copy(tabv, tab, lsem.at[5])
    lc.start()
    enc_load.wait()
    lc.wait()

    def give_rows(i, peer):
        return remote(send.at[i], slots.at[i, mine], ssend.at[i], srecv.at[i], seq=peer)

    def share_rows(i):
        part = slots.at[i, mine]
        return remote(part, part, fsend.at[i], frecv.at[i], head=other)

    for i in range(1, PEERS):
        place = jnp.maximum(tab[opposite(i), 0, me] - 1, 0)
        send[i] = enc[place, mine, :]
        give_rows(i, plane_peer(x, y, i)).start()
    slots[0] = enc[jnp.maximum(tab[0, 0, me] - 1, 0)]
    for c in weights:
        c.wait()

    def project(j):
        block = slots[pl.ds(2 * j, 2)].reshape(2 * NROWS, D_ENC)
        for g in range(2 * GROUPS):
            cols = pl.ds(g * STEP, STEP)
            kv[pl.ds(2 * j, 2), :, cols] = nn(block, w[:, cols]).astype(BF).reshape(2, NROWS, STEP)
        enct[2 * j] = block[:NROWS].T
        enct[2 * j + 1] = block[NROWS:].T

    def arrive(i):
        give_rows(i, after).wait_recv()
        share_rows(i).start()

    arrive(1)

    def pair(j):
        @pl.when(j < PEERS // 2 - 1)
        def _():
            arrive(2 * j + 2)
            arrive(2 * j + 3)

        @pl.when(j > 0)
        def _():
            share_rows(2 * j).wait_recv()

        share_rows(2 * j + 1).wait_recv()
        project(j)

    each(0, PEERS // 2, pair)
    for c in loads:
        c.wait()
    for c in halos:
        c.wait()
    for r in range(REFS):
        refs_t[:, pl.ds(r * NROWS, NROWS)] = enct[kin[r]]

    move = shift_matrix(ROWS, ROWS + RIM, RIM - 1)
    inside = lax.broadcasted_iota(jnp.int32, (ROWS, ROWS + RIM), 1) < jnp.where(me == PEERS - 1, ROWS, ROWS + RIM)
    move = jnp.where(inside, up(move), 0.0).astype(BF)
    col = lax.broadcasted_iota(jnp.int32, (SPAN, 2 * NROWS), 1)

    def first_a(g, k):
        xp = lax.rem(x + k, SIDE)
        return remote(dw.at[g, 0, xp], r1a.at[g, k - 1], send1a.at[g, k - 1], recv1a.at[g, k - 1], seq=xp * SIDE + y)

    def first_b(g, k):
        yp = lax.rem(y + k, SIDE)
        return remote(dw.at[g, 1, :, yp], r1b.at[g, k - 1], send1b.at[g, k - 1], recv1b.at[g, k - 1], seq=x * SIDE + yp)

    def second_a(k):
        yp = lax.rem(y + k, SIDE)
        return remote(s2a.at[:, yp], r2a.at[k - 1], send2a.at[k - 1], recv2a.at[k - 1], seq=x * SIDE + yp)

    def second_b(k):
        xp = lax.rem(x + k, SIDE)
        return remote(s2b.at[:, xp], r2b.at[k - 1], send2b.at[k - 1], recv2b.at[k - 1], seq=xp * SIDE + y)

    def sum_first(g):
        for k in (1, 2, 3):
            first_a(g, k).wait()
            first_b(g, k).wait()
        for j in range(SIDE):
            s2a[g - 1, j] = (up(dw[g, 0, x, j]) + up(r1a[g, 0, j]) + up(r1a[g, 1, j]) + up(r1a[g, 2, j])).astype(BF)
            s2b[g - 1, j] = (up(dw[g, 1, j, y]) + up(r1b[g, 0, j]) + up(r1b[g, 1, j]) + up(r1b[g, 2, j])).astype(BF)

    m = lax.broadcasted_iota(jnp.int32, (DEPTH * 8, SHARE), 0)
    e = lax.broadcasted_iota(jnp.int32, (DEPTH * 8, SHARE), 1)
    spread = jnp.logical_and(m // 8 * PIECE + m % 8 == e, m % 8 < PIECE).astype(F32).astype(BF)

    def level_first(k):
        zp = lax.rem(level + k, DEPTH)
        return remote(zs.at[zp], zr.at[k], zsend.at[k], zrecv.at[k], dp=zp)

    def group(g, first=False):
        cols = pl.ds(pl.multiple_of(g * STEP, STEP), STEP)
        cols_v = pl.ds(pl.multiple_of(g * STEP + FEAT, STEP), STEP)
        qs = nn(move, qx[:, cols]).astype(BF)
        do = nn(move, dx[:, cols]).astype(BF)
        units = [(c, h) for c in range(REFS // 2) for h in range(STEP // HD)]

        def cut(a, c, h):
            return a[c * SPAN : (c + 1) * SPAN, h * HD : (h + 1) * HD]

        def head(h, base=0):
            return pl.ds(pl.multiple_of(g * STEP + h * HD + base, HD), HD)

        def both(c, h, base):
            return jnp.concatenate([kv[kin[2 * c + n], :, head(h, base)] for n in range(2)], axis=0)

        k_u = [both(c, h, 0) for c, h in units]
        v_u = [both(c, h, FEAT) for c, h in units]
        q_u = [cut(qs, c, h) for c, h in units]
        d_u = [cut(do, c, h) for c, h in units]
        scores = [nt(q, k) * scale for q, k in zip(q_u, k_u)]
        dprobs = [nt(d, v) for d, v in zip(d_u, v_u)]
        probs_b, ds_b = [], []
        for (c, h), s, dp in zip(units, scores, dprobs):
            s = jnp.where(col < cnt_ref[0, c] * NROWS, s, -1e30)
            e = jnp.exp(s - jnp.max(s, axis=-1, keepdims=True))
            p = e / jnp.sum(e, axis=-1, keepdims=True)
            pb = p.astype(BF)
            delta = jnp.sum(up(pb) * dp, axis=-1, keepdims=True)
            probs_b.append(pb)
            ds_b.append((p * (dp - delta)).astype(BF))
        for (c, h), q, d, k, pb, ds in zip(units, q_u, d_u, k_u, probs_b, ds_b):
            two = pl.ds(2 * c, 2)
            gs[pl.ds(c * SPAN, SPAN), head(h)] = (nn(ds, k) * scale).astype(BF)
            dkv[two, :, head(h)] = (tn(ds, q) * scale).astype(BF).reshape(2, NROWS, HD)
            dkv[two, :, head(h, FEAT)] = tn(pb, d).astype(BF).reshape(2, NROWS, HD)
        dk = dkv[:, :, cols].reshape(REFS * NROWS, STEP)
        dv = dkv[:, :, cols_v].reshape(REFS * NROWS, STEP)
        dw[g, 0] = nn(refs_t[...], dk).astype(BF).reshape(SIDE, SIDE, SHARE, STEP)
        dw[g, 1] = nn(refs_t[...], dv).astype(BF).reshape(SIDE, SIDE, SHARE, STEP)
        if first:
            for n in range(2):
                for i in range(PEERS):
                    zs[:, n, i] = nn(spread, dw[0, n, i // SIDE, i % SIDE]).astype(BF).reshape(DEPTH, 8, STEP)
            for k in (4, 3, 5, 2, 6, 1, 7):
                level_first(k).start()
        else:
            for k in (2, 1, 3):
                first_a(g, k).start()
                first_b(g, k).start()

    group(0, first=True)
    each(1, GROUPS, group)
    halo = remote(gs.at[pl.ds(ROWS - RIM, RIM)], prev, prev_sem.at[0], prev_sem.at[1], seq=after)
    halo.start()

    con[...] = nt(dkv[:, theirs, :].reshape(REFS * HALF, 2 * FEAT), w[...]).reshape(REFS, HALF, D_ENC)
    swap = remote(con, hbuf, swap_sem.at[0], swap_sem.at[1], head=other)
    swap.start()
    own = nt(dkv[:, mine, :].reshape(REFS * HALF, 2 * FEAT), w[...]).reshape(REFS, HALF, D_ENC)
    swap.wait()
    half[...] = (own + hbuf[...]).astype(BF)
    each(1, GROUPS, sum_first)
    for k in (2, 1, 3):
        second_a(k).start()
        second_b(k).start()

    def ref_for(peer):
        found = jnp.int32(0)
        for r in range(REFS):
            found = jnp.where(owners[r] == peer, jnp.int32(r), found)
        return found

    each(1, PEERS, lambda i: give_rows(i, after).wait_send())

    def return_rows(i, peer):
        return remote(send.at[i], recv.at[i], rsend.at[i], rrecv.at[i], seq=peer)

    for i in range(1, PEERS):
        peer = plane_peer(x, y, i)
        send[i] = half[ref_for(peer)]
        return_rows(i, peer).start()
    recv[0] = half[ref_for(me)]

    halo.wait()
    old = jnp.where(me == 0, 0.0, 1.0)
    ext = jnp.concatenate([(up(prev[...]) * old).astype(BF), gs[...]], axis=0)
    gqv[...] = nn(shift_matrix(ROWS, ROWS + RIM, 1), ext).astype(BF)
    gq_out = pltpu.make_async_copy(gqv, gq_hbm, osem.at[0])
    gq_out.start()

    for k in (1, 2, 3):
        second_a(k).wait()
        second_b(k).wait()
    for g in range(1, GROUPS):
        own_a = up(dw[g, 0, x, y]) + up(r1a[g, 0, y]) + up(r1a[g, 1, y]) + up(r1a[g, 2, y])
        own_b = up(dw[g, 1, x, y]) + up(r1b[g, 0, x]) + up(r1b[g, 1, x]) + up(r1b[g, 2, x])
        t_a = (own_a + up(r2a[0, g - 1]) + up(r2a[1, g - 1]) + up(r2a[2, g - 1])).astype(BF)
        t_b = (own_b + up(r2b[0, g - 1]) + up(r2b[1, g - 1]) + up(r2b[2, g - 1])).astype(BF)
        cols = pl.ds((g - 1) * STEP, STEP)
        s3[:, 0, :, cols] = nn(spread, t_a).astype(BF).reshape(DEPTH, 8, STEP)
        s3[:, 1, :, cols] = nn(spread, t_b).astype(BF).reshape(DEPTH, 8, STEP)

    def third(k):
        zp = lax.rem(level + k, DEPTH)
        return remote(s3.at[zp], r3.at[k], send3.at[k], recv3.at[k], dp=zp)

    for k in (4, 3, 5, 2, 6, 1, 7):
        third(k).start()

    each(1, DEPTH, lambda k: level_first(k).wait())

    def sum_levels(i):
        for n in range(2):
            part = up(zs[level, n, i])
            for k in range(1, DEPTH):
                part = part + up(zr[k, n, i])
            zt[i, n] = part.astype(BF)

    each(0, PEERS, sum_levels)

    def plane_last(i, peer):
        return remote(zt.at[peer], zu.at[i], tsend.at[i], trecv.at[i], seq=peer)

    for i in range(1, PEERS):
        plane_last(i, plane_peer(x, y, i)).start()

    place = lax.broadcasted_iota(jnp.int32, (OWNED * HALF, 2 * HALF), 0)
    slot = lax.broadcasted_iota(jnp.int32, (OWNED * HALF, 2 * HALF), 1)
    pick = []
    for t in range(PEERS // 2):
        lo = (tab[2 * t, 0, me] - 1) * HALF
        hi = (tab[2 * t + 1, 0, me] - 1) * HALF
        target = jnp.where(slot < HALF, slot + lo, slot - HALF + hi)
        live = jnp.where(slot < HALF, lo, hi) >= 0
        pick.append(jnp.logical_and(place == target, live).astype(F32).astype(BF))
    pick = jnp.concatenate(pick, axis=1)
    each(1, PEERS, lambda i: return_rows(i, after).wait_recv())
    total = nn(pick, recv[...].reshape(PEERS * HALF, D_ENC))
    ohalf[...] = total.astype(BF).reshape(OWNED, HALF, D_ENC)
    back = remote(ohalf, ge_hbm.at[:, mine], back_sem.at[0], back_sem.at[1], head=other)
    back.start()
    ge_out = pltpu.make_async_copy(ohalf, ge_hbm.at[:, mine], osem.at[1])
    ge_out.start()

    each(1, DEPTH, lambda k: third(k).wait())
    final = up(s3[level])
    for k in range(1, DEPTH):
        final = final + up(r3[k])
    each(1, PEERS, lambda i: plane_last(i, after).wait())
    zero = up(zt[me])
    for i in range(1, PEERS):
        zero = zero + up(zu[i])
    for n in range(2):
        gw_ref[:, n, pl.ds(0, STEP)] = zero[n, :PIECE]
        gw_ref[:, n, pl.ds(STEP, FEAT - STEP)] = final[n, :PIECE]

    each(1, PEERS, lambda i: ask(i, after).wait_send())
    each(1, PEERS, lambda i: share_rows(i).wait_send())
    each(1, PEERS, lambda i: return_rows(i, after).wait_send())
    gq_out.wait()
    ge_out.wait()
    back.wait()


def finish_kernel(gq, ge, gw, gq_out, ge_out, gw_out):
    gq_out[...] = gq[...]
    ge_out[...] = ge[...]
    gw_out[...] = gw[...]


def body(queries, out_grad, encodings, owner_map, nbr_count, key_weight, value_weight):
    vm = pl.BlockSpec(memory_space=pltpu.VMEM)
    sm = pl.BlockSpec(memory_space=pltpu.SMEM)
    hbm = pl.BlockSpec(memory_space=pl.ANY)
    dma = pltpu.SemaphoreType.DMA

    def bf(*shape):
        return pltpu.VMEM(shape, BF)

    gq, ge, gw = pl.pallas_call(
        kernel,
        out_shape=(
            jax.ShapeDtypeStruct((ROWS, FEAT), BF),
            jax.ShapeDtypeStruct((OWNED, NROWS, D_ENC), BF),
            jax.ShapeDtypeStruct((PIECE, 2, FEAT), F32),
        ),
        in_specs=[sm, sm, hbm, hbm, hbm, hbm, hbm],
        out_specs=(hbm, hbm, vm),
        scratch_shapes=[
            bf(OWNED, NROWS, D_ENC),
            bf(D_ENC, 2 * FEAT),
            bf(ROWS + RIM, FEAT),
            bf(ROWS + RIM, FEAT),
            pltpu.VMEM((1, 128), jnp.int32),
            pltpu.VMEM((PEERS, 1, 128), jnp.int32),
            pltpu.SMEM((PEERS, 1, 128), jnp.int32),
            bf(PEERS, HALF, D_ENC),
            bf(PEERS, NROWS, D_ENC),
            bf(PEERS, NROWS, 2 * FEAT),
            bf(PEERS, D_ENC, NROWS),
            bf(D_ENC, REFS * NROWS),
            bf(REFS, NROWS, 2 * FEAT),
            pltpu.VMEM((REFS, HALF, D_ENC), F32),
            pltpu.VMEM((REFS, HALF, D_ENC), F32),
            bf(REFS, HALF, D_ENC),
            bf(PEERS, HALF, D_ENC),
            bf(OWNED, HALF, D_ENC),
            bf(ROWS, FEAT),
            bf(RIM, FEAT),
            bf(ROWS, FEAT),
            bf(GROUPS, 2, SIDE, SIDE, SHARE, STEP),
            bf(GROUPS, SIDE - 1, SIDE, SHARE, STEP),
            bf(GROUPS, SIDE - 1, SIDE, SHARE, STEP),
            bf(GROUPS - 1, SIDE, SHARE, STEP),
            bf(GROUPS - 1, SIDE, SHARE, STEP),
            bf(SIDE - 1, GROUPS - 1, SHARE, STEP),
            bf(SIDE - 1, GROUPS - 1, SHARE, STEP),
            bf(DEPTH, 2, 8, FEAT - STEP),
            bf(DEPTH, 2, 8, FEAT - STEP),
            bf(DEPTH, 2, PEERS, 8, STEP),
            bf(DEPTH, 2, PEERS, 8, STEP),
            bf(PEERS, 2, 8, STEP),
            bf(PEERS, 2, 8, STEP),
            dma((6,)), dma((2,)),
            dma((PEERS,)), dma((PEERS,)), dma((PEERS,)), dma((PEERS,)), dma((PEERS,)), dma((PEERS,)),
            dma((2,)), dma((2,)), dma((2,)),
            dma((PEERS,)), dma((PEERS,)), dma((2,)), dma((2,)),
            dma((GROUPS, 3)), dma((GROUPS, 3)), dma((GROUPS, 3)), dma((GROUPS, 3)),
            dma((3,)), dma((3,)), dma((3,)), dma((3,)),
            dma((DEPTH,)), dma((DEPTH,)), dma((DEPTH,)), dma((DEPTH,)), dma((PEERS,)), dma((PEERS,)),
        ],
        compiler_params=pltpu.CompilerParams(
            collective_id=0, has_side_effects=True, vmem_limit_bytes=VMEM_LIMIT
        ),
        name="spans",
    )(
        jnp.swapaxes(owner_map, 1, 2), nbr_count, encodings.reshape(OWNED, NROWS, D_ENC),
        queries[0], out_grad[0], key_weight, value_weight,
    )
    parts = (
        pl.BlockSpec((ROWS // 4, FEAT), lambda n: (n, 0)),
        pl.BlockSpec((OWNED // 4, NROWS, D_ENC), lambda n: (n, 0, 0)),
        pl.BlockSpec((PIECE, 2, FEAT), lambda n: (0, 0, 0)),
    )
    gq, ge, gw = pl.pallas_call(
        finish_kernel,
        grid=(4,),
        out_shape=tuple(jax.ShapeDtypeStruct(a.shape, a.dtype) for a in (gq, ge, gw)),
        in_specs=parts,
        out_specs=parts,
        name="finish",
    )(gq, ge, gw)
    return gq[None], ge.reshape(1, OWNED * NROWS, D_ENC), gw


def solution(mesh):
    return jax.shard_map(
        body,
        mesh=mesh,
        in_specs=(
            P("dp", "seq", "head"),
            P("dp", "seq", "head"),
            P("dp", "seq", None),
            P("dp", "seq", None),
            P("dp", "seq"),
            P(None, "head"),
            P(None, "head"),
        ),
        out_specs=(P("dp", "seq", "head"), P("dp", "seq", None), P(("seq", "dp"), None, "head")),
        check_vma=False,
    )
```

```python
import functools
import math

import jax
import jax.numpy as jnp
from jax import lax
from jax.experimental import pallas as pl
from jax.experimental.pallas import tpu as pltpu
from jax.sharding import PartitionSpec as P

MESH = pl.DeviceIdType.MESH
HD = 128
SPAN = 64
NROWS = 128
REFS = 8
SIDE = 4
PEERS = SIDE * SIDE
DEPTH = 8
HALF = NROWS // 2
OWNED = 8
D_ENC = 896
FEAT = 1024
ROWS = 256
RIM = 64
STEP = 256
GROUPS = FEAT // STEP
Z_GROUP = 2
XY_GROUPS = [0, 1, 3]
SHARE = D_ENC // PEERS
PIECE = SHARE // DEPTH
VMEM_LIMIT = 58 << 20
BF = jnp.bfloat16
F32 = jnp.float32


def ring(step):
    return min(step, SIDE - step)


STEPS = sorted(
    [(dx, dy) for dx in range(SIDE) for dy in range(SIDE)],
    key=lambda s: -(ring(s[0]) + ring(s[1])) if s != (0, 0) else -9,
)


def plane_place():
    me = lax.axis_index("seq")
    return me, lax.div(me, SIDE), lax.rem(me, SIDE)


def plane_peer(x, y, i):
    dx, dy = STEPS[i]
    return lax.rem(x + dx, SIDE) * SIDE + lax.rem(y + dy, SIDE)


def opposite(i):
    dx, dy = STEPS[i]
    return STEPS.index((-dx % SIDE, -dy % SIDE))


def each(start, stop, step):
    def one(k, carry):
        step(k)
        return carry

    lax.fori_loop(start, stop, one, 0)


def up(a):
    return a.astype(F32)


def remote(src, dst, send_sem, recv_sem, **where):
    return pltpu.make_async_remote_copy(
        src_ref=src,
        dst_ref=dst,
        send_sem=send_sem,
        recv_sem=recv_sem,
        device_id=where,
        device_id_type=MESH,
    )


def greet(barrier, **where):
    pl.semaphore_signal(barrier, inc=1, device_id=where, device_id_type=MESH)


def nt(a, b):
    return lax.dot_general(a, b, (((1,), (1,)), ((), ())), preferred_element_type=F32)


def tn(a, b):
    return lax.dot_general(a, b, (((0,), (0,)), ((), ())), preferred_element_type=F32)


def nn(a, b):
    return jnp.dot(a, b, preferred_element_type=F32)


def shift_matrix(rows, columns, by):
    i = lax.broadcasted_iota(jnp.int32, (rows, columns), 0)
    e = lax.broadcasted_iota(jnp.int32, (rows, columns), 1)
    return (e == i + by).astype(F32).astype(BF)


def kernel(
    map_ref, cnt_ref, enc_hbm, q_hbm, d_hbm, wk_hbm, wv_hbm,
    gq_hbm, ge_hbm, gw_ref,
    enc, w, qx, dx, asked, tabv, tab, send, slots, kv, enct, refs_t,
    dkv, con, hbuf, half, recv, ohalf, gs, prev, gqv, dw, r1a, r1b, s2a, s2b, r2a, r2b, s3, r3, zs, zr, zt, zu,
    lsem, osem, isend, irecv, ssend, srecv, fsend, frecv, halo_send, halo_recv,
    swap_sem, rsend, rrecv, back_sem, prev_sem,
    send1a, recv1a, send1b, recv1b, send2a, recv2a, send2b, recv2b, send3, recv3, zsend, zrecv, tsend, trecv,
):
    me, x, y = plane_place()
    core = lax.axis_index("head")
    level = lax.axis_index("dp")
    other = 1 - core
    scale = 1.0 / math.sqrt(HD)
    mine = pl.ds(pl.multiple_of(core * HALF, HALF), HALF)
    theirs = pl.ds(pl.multiple_of(other * HALF, HALF), HALF)
    before = lax.rem(me + PEERS - 1, PEERS)
    after = lax.rem(me + 1, PEERS)

    barrier = pltpu.get_barrier_semaphore()
    for i in range(1, PEERS):
        greet(barrier, seq=plane_peer(x, y, i))
    greet(barrier, head=other)
    each(1, DEPTH, lambda k: greet(barrier, dp=lax.rem(level + k, DEPTH)))

    enc_load = pltpu.make_async_copy(enc_hbm, enc, lsem.at[0])
    loads = [
        pltpu.make_async_copy(q_hbm, qx.at[pl.ds(0, ROWS)], lsem.at[1]),
        pltpu.make_async_copy(d_hbm, dx.at[pl.ds(0, ROWS)], lsem.at[2]),
    ]
    weights = [
        pltpu.make_async_copy(wk_hbm, w.at[:, pl.ds(0, FEAT)], lsem.at[3]),
        pltpu.make_async_copy(wv_hbm, w.at[:, pl.ds(FEAT, FEAT)], lsem.at[4]),
    ]
    for c in [enc_load] + weights + loads:
        c.start()

    lane = lax.broadcasted_iota(jnp.int32, (1, 128), 1)
    row = jnp.zeros((1, 128), jnp.int32)
    owners, kin = [], []
    for r in range(REFS):
        entry = map_ref[0, r % 2, r // 2]
        owner = lax.div(entry, OWNED)
        row = jnp.where(lane == owner, lax.rem(entry, OWNED) + 1, row)
        owners.append(owner)
        kx = lax.rem(x - lax.div(owner, SIDE) + SIDE, SIDE)
        ky = lax.rem(y - lax.rem(owner, SIDE) + SIDE, SIDE)
        found = jnp.int32(0)
        for i in range(1, PEERS):
            found = jnp.where(kx * SIDE + ky == STEPS[i][0] * SIDE + STEPS[i][1], jnp.int32(i), found)
        kin.append(found)
    asked[...] = row
    tabv[0] = row
    pl.semaphore_wait(barrier, PEERS + DEPTH - 1)

    def ask(i, peer):
        return remote(asked, tabv.at[i], isend.at[i], irecv.at[i], seq=peer)

    for i in range(1, PEERS):
        ask(i, plane_peer(x, y, i)).start()
    halos = [
        remote(q_hbm.at[pl.ds(0, RIM)], qx.at[pl.ds(ROWS, RIM)], halo_send.at[0], halo_recv.at[0], seq=before),
        remote(d_hbm.at[pl.ds(0, RIM)], dx.at[pl.ds(ROWS, RIM)], halo_send.at[1], halo_recv.at[1], seq=before),
    ]
    for c in halos:
        c.start()
    each(1, PEERS, lambda i: ask(i, after).wait_recv())
    lc = pltpu.make_async_copy(tabv, tab, lsem.at[5])
    lc.start()
    enc_load.wait()
    lc.wait()

    def give_rows(i, peer):
        return remote(send.at[i], slots.at[i, mine], ssend.at[i], srecv.at[i], seq=peer)

    def share_rows(i):
        part = slots.at[i, mine]
        return remote(part, part, fsend.at[i], frecv.at[i], head=other)

    for i in range(1, PEERS):
        place = jnp.maximum(tab[opposite(i), 0, me] - 1, 0)
        send[i] = enc[place, mine, :]
        give_rows(i, plane_peer(x, y, i)).start()
    slots[0] = enc[jnp.maximum(tab[0, 0, me] - 1, 0)]
    for c in weights:
        c.wait()

    def project(j):
        block = slots[pl.ds(2 * j, 2)].reshape(2 * NROWS, D_ENC)
        for g in range(2 * GROUPS):
            cols = pl.ds(g * STEP, STEP)
            kv[pl.ds(2 * j, 2), :, cols] = nn(block, w[:, cols]).astype(BF).reshape(2, NROWS, STEP)
        enct[2 * j] = block[:NROWS].T
        enct[2 * j + 1] = block[NROWS:].T

    def arrive(i):
        give_rows(i, after).wait_recv()
        share_rows(i).start()

    arrive(1)

    def pair(j):
        @pl.when(j < PEERS // 2 - 1)
        def _():
            arrive(2 * j + 2)
            arrive(2 * j + 3)

        @pl.when(j > 0)
        def _():
            share_rows(2 * j).wait_recv()

        share_rows(2 * j + 1).wait_recv()
        project(j)

    each(0, PEERS // 2, pair)
    for c in loads:
        c.wait()
    for c in halos:
        c.wait()
    for r in range(REFS):
        refs_t[:, pl.ds(r * NROWS, NROWS)] = enct[kin[r]]

    move = shift_matrix(ROWS, ROWS + RIM, RIM - 1)
    inside = lax.broadcasted_iota(jnp.int32, (ROWS, ROWS + RIM), 1) < jnp.where(me == PEERS - 1, ROWS, ROWS + RIM)
    move = jnp.where(inside, up(move), 0.0).astype(BF)
    col = lax.broadcasted_iota(jnp.int32, (SPAN, 2 * NROWS), 1)

    def first_a(g, k):
        xp = lax.rem(x + k, SIDE)
        return remote(dw.at[g, 0, xp], r1a.at[g, k - 1], send1a.at[g, k - 1], recv1a.at[g, k - 1], seq=xp * SIDE + y)

    def first_b(g, k):
        yp = lax.rem(y + k, SIDE)
        return remote(dw.at[g, 1, :, yp], r1b.at[g, k - 1], send1b.at[g, k - 1], recv1b.at[g, k - 1], seq=x * SIDE + yp)

    def second_a(k):
        yp = lax.rem(y + k, SIDE)
        return remote(s2a.at[:, yp], r2a.at[k - 1], send2a.at[k - 1], recv2a.at[k - 1], seq=x * SIDE + yp)

    def second_b(k):
        xp = lax.rem(x + k, SIDE)
        return remote(s2b.at[:, xp], r2b.at[k - 1], send2b.at[k - 1], recv2b.at[k - 1], seq=xp * SIDE + y)

    def sum_first(n):
        g = n + lax.div(n, 2)
        for k in (1, 2, 3):
            first_a(g, k).wait()
            first_b(g, k).wait()
        for j in range(SIDE):
            s2a[n, j] = (up(dw[g, 0, x, j]) + up(r1a[g, 0, j]) + up(r1a[g, 1, j]) + up(r1a[g, 2, j])).astype(BF)
            s2b[n, j] = (up(dw[g, 1, j, y]) + up(r1b[g, 0, j]) + up(r1b[g, 1, j]) + up(r1b[g, 2, j])).astype(BF)

    m = lax.broadcasted_iota(jnp.int32, (DEPTH * 8, SHARE), 0)
    e = lax.broadcasted_iota(jnp.int32, (DEPTH * 8, SHARE), 1)
    spread = jnp.logical_and(m // 8 * PIECE + m % 8 == e, m % 8 < PIECE).astype(F32).astype(BF)

    def level_first(k):
        zp = lax.rem(level + k, DEPTH)
        return remote(zs.at[zp], zr.at[k], zsend.at[k], zrecv.at[k], dp=zp)

    def halo_cols(g):
        cols = pl.ds(pl.multiple_of(g * STEP, STEP), STEP)
        return remote(gs.at[pl.ds(ROWS - RIM, RIM), cols], prev.at[:, cols], prev_sem.at[0, g], prev_sem.at[1, g], seq=after)

    def group(g):
        cols = pl.ds(pl.multiple_of(g * STEP, STEP), STEP)
        cols_v = pl.ds(pl.multiple_of(g * STEP + FEAT, STEP), STEP)
        qs = nn(move, qx[:, cols]).astype(BF)
        do = nn(move, dx[:, cols]).astype(BF)
        units = [(c, h) for c in range(REFS // 2) for h in range(STEP // HD)]

        def cut(a, c, h):
            return a[c * SPAN : (c + 1) * SPAN, h * HD : (h + 1) * HD]

        def head(h, base=0):
            return pl.ds(pl.multiple_of(g * STEP + h * HD + base, HD), HD)

        def both(c, h, base):
            return jnp.concatenate([kv[kin[2 * c + n], :, head(h, base)] for n in range(2)], axis=0)

        k_u = [both(c, h, 0) for c, h in units]
        v_u = [both(c, h, FEAT) for c, h in units]
        q_u = [cut(qs, c, h) for c, h in units]
        d_u = [cut(do, c, h) for c, h in units]
        scores = [nt(q, k) * scale for q, k in zip(q_u, k_u)]
        dprobs = [nt(d, v) for d, v in zip(d_u, v_u)]
        probs_b, ds_b = [], []
        for (c, h), s, dp in zip(units, scores, dprobs):
            s = jnp.where(col < cnt_ref[0, c] * NROWS, s, -1e30)
            e = jnp.exp(s - jnp.max(s, axis=-1, keepdims=True))
            p = e / jnp.sum(e, axis=-1, keepdims=True)
            pb = p.astype(BF)
            delta = jnp.sum(up(pb) * dp, axis=-1, keepdims=True)
            probs_b.append(pb)
            ds_b.append((p * (dp - delta)).astype(BF))
        for (c, h), q, d, k, pb, ds in zip(units, q_u, d_u, k_u, probs_b, ds_b):
            two = pl.ds(2 * c, 2)
            gs[pl.ds(c * SPAN, SPAN), head(h)] = (nn(ds, k) * scale).astype(BF)
            dkv[two, :, head(h)] = (tn(ds, q) * scale).astype(BF).reshape(2, NROWS, HD)
            dkv[two, :, head(h, FEAT)] = tn(pb, d).astype(BF).reshape(2, NROWS, HD)
        dk = dkv[:, :, cols].reshape(REFS * NROWS, STEP)
        dv = dkv[:, :, cols_v].reshape(REFS * NROWS, STEP)
        plane = g != Z_GROUP
        halo_cols(g).start()
        dw[g, 0] = nn(refs_t[...], dk).astype(BF).reshape(SIDE, SIDE, SHARE, STEP)

        @pl.when(plane)
        def _():
            for k in (2, 1, 3):
                first_a(g, k).start()

        dw[g, 1] = nn(refs_t[...], dv).astype(BF).reshape(SIDE, SIDE, SHARE, STEP)

        @pl.when(plane)
        def _():
            for k in (2, 1, 3):
                first_b(g, k).start()

        @pl.when(jnp.logical_not(plane))
        def _():
            for n in range(2):
                for i in range(PEERS):
                    piece = nn(spread, dw[Z_GROUP, n, i // SIDE, i % SIDE])
                    zs[:, n, i] = piece.astype(BF).reshape(DEPTH, 8, STEP)
            for k in (4, 3, 5, 2, 6, 1, 7):
                level_first(k).start()

    each(0, GROUPS, group)

    con[...] = nt(dkv[:, theirs, :].reshape(REFS * HALF, 2 * FEAT), w[...]).reshape(REFS, HALF, D_ENC)
    swap = remote(con, hbuf, swap_sem.at[0], swap_sem.at[1], head=other)
    swap.start()
    own = nt(dkv[:, mine, :].reshape(REFS * HALF, 2 * FEAT), w[...]).reshape(REFS, HALF, D_ENC)
    swap.wait()
    half[...] = (own + hbuf[...]).astype(BF)

    def ref_for(peer):
        found = jnp.int32(0)
        for r in range(REFS):
            found = jnp.where(owners[r] == peer, jnp.int32(r), found)
        return found

    each(1, PEERS, lambda i: give_rows(i, after).wait_send())

    def return_rows(i, peer):
        return remote(send.at[i], recv.at[i], rsend.at[i], rrecv.at[i], seq=peer)

    for i in range(1, 9):
        peer = plane_peer(x, y, i)
        send[i] = half[ref_for(peer)]
        return_rows(i, peer).start()
    recv[0] = half[ref_for(me)]
    each(0, GROUPS - 1, sum_first)
    for k in (2, 1, 3):
        second_a(k).start()
        second_b(k).start()
    for i in range(9, PEERS):
        peer = plane_peer(x, y, i)
        send[i] = half[ref_for(peer)]
        return_rows(i, peer).start()

    each(0, GROUPS, lambda g: halo_cols(g).wait())
    old = jnp.where(me == 0, 0.0, 1.0)
    ext = jnp.concatenate([(up(prev[...]) * old).astype(BF), gs[...]], axis=0)
    gqv[...] = nn(shift_matrix(ROWS, ROWS + RIM, 1), ext).astype(BF)
    gq_out = pltpu.make_async_copy(gqv, gq_hbm, osem.at[0])
    gq_out.start()

    for k in (1, 2, 3):
        second_a(k).wait()
        second_b(k).wait()
    for n, g in enumerate(XY_GROUPS):
        own_a = up(dw[g, 0, x, y]) + up(r1a[g, 0, y]) + up(r1a[g, 1, y]) + up(r1a[g, 2, y])
        own_b = up(dw[g, 1, x, y]) + up(r1b[g, 0, x]) + up(r1b[g, 1, x]) + up(r1b[g, 2, x])
        t_a = (own_a + up(r2a[0, n]) + up(r2a[1, n]) + up(r2a[2, n])).astype(BF)
        t_b = (own_b + up(r2b[0, n]) + up(r2b[1, n]) + up(r2b[2, n])).astype(BF)
        cols = pl.ds(n * STEP, STEP)
        s3[:, 0, :, cols] = nn(spread, t_a).astype(BF).reshape(DEPTH, 8, STEP)
        s3[:, 1, :, cols] = nn(spread, t_b).astype(BF).reshape(DEPTH, 8, STEP)

    def third(k):
        zp = lax.rem(level + k, DEPTH)
        return remote(s3.at[zp], r3.at[k], send3.at[k], recv3.at[k], dp=zp)

    for k in (4, 3, 5, 2, 6, 1, 7):
        third(k).start()

    each(1, DEPTH, lambda k: level_first(k).wait())

    def sum_levels(i):
        for n in range(2):
            part = up(zs[level, n, i])
            for k in range(1, DEPTH):
                part = part + up(zr[k, n, i])
            zt[i, n] = part.astype(BF)

    each(0, PEERS, sum_levels)

    def plane_last(i, peer):
        return remote(zt.at[peer], zu.at[i], tsend.at[i], trecv.at[i], seq=peer)

    for i in range(1, PEERS):
        plane_last(i, plane_peer(x, y, i)).start()

    place = lax.broadcasted_iota(jnp.int32, (OWNED * HALF, 2 * HALF), 0)
    slot = lax.broadcasted_iota(jnp.int32, (OWNED * HALF, 2 * HALF), 1)
    pick = []
    for t in range(PEERS // 2):
        lo = (tab[2 * t, 0, me] - 1) * HALF
        hi = (tab[2 * t + 1, 0, me] - 1) * HALF
        target = jnp.where(slot < HALF, slot + lo, slot - HALF + hi)
        live = jnp.where(slot < HALF, lo, hi) >= 0
        pick.append(jnp.logical_and(place == target, live).astype(F32).astype(BF))
    early = PEERS // 2
    each(1, early, lambda i: return_rows(i, after).wait_recv())
    con[...] = nn(
        jnp.concatenate(pick[: early // 2], axis=1), recv[:early].reshape(early * HALF, D_ENC)
    ).reshape(OWNED, HALF, D_ENC)
    each(early, PEERS, lambda i: return_rows(i, after).wait_recv())
    late = nn(jnp.concatenate(pick[early // 2 :], axis=1), recv[early:].reshape(early * HALF, D_ENC))
    ohalf[...] = (con[...] + late.reshape(OWNED, HALF, D_ENC)).astype(BF)
    back = remote(ohalf, ge_hbm.at[:, mine], back_sem.at[0], back_sem.at[1], head=other)
    back.start()
    ge_out = pltpu.make_async_copy(ohalf, ge_hbm.at[:, mine], osem.at[1])
    ge_out.start()

    each(1, DEPTH, lambda k: third(k).wait())
    final = up(s3[level])
    for k in range(1, DEPTH):
        final = final + up(r3[k])
    each(1, PEERS, lambda i: plane_last(i, after).wait())
    zero = up(zt[me])
    for i in range(1, PEERS):
        zero = zero + up(zu[i])
    for t in range(2):
        gw_ref[:, t, pl.ds(Z_GROUP * STEP, STEP)] = zero[t, :PIECE]
        for n, g in enumerate(XY_GROUPS):
            gw_ref[:, t, pl.ds(g * STEP, STEP)] = final[t, :PIECE, n * STEP : (n + 1) * STEP]

    each(1, PEERS, lambda i: ask(i, after).wait_send())
    each(1, PEERS, lambda i: share_rows(i).wait_send())
    each(1, PEERS, lambda i: return_rows(i, after).wait_send())
    gq_out.wait()
    ge_out.wait()
    back.wait()


def finish_kernel(gq, ge, gw, gq_out, ge_out, gw_out):
    gq_out[...] = gq[...]
    ge_out[...] = ge[...]
    gw_out[...] = gw[...]


def body(queries, out_grad, encodings, owner_map, nbr_count, key_weight, value_weight):
    vm = pl.BlockSpec(memory_space=pltpu.VMEM)
    sm = pl.BlockSpec(memory_space=pltpu.SMEM)
    hbm = pl.BlockSpec(memory_space=pl.ANY)
    dma = pltpu.SemaphoreType.DMA

    def bf(*shape):
        return pltpu.VMEM(shape, BF)

    gq, ge, gw = pl.pallas_call(
        kernel,
        out_shape=(
            jax.ShapeDtypeStruct((ROWS, FEAT), BF),
            jax.ShapeDtypeStruct((OWNED, NROWS, D_ENC), BF),
            jax.ShapeDtypeStruct((PIECE, 2, FEAT), F32),
        ),
        in_specs=[sm, sm, hbm, hbm, hbm, hbm, hbm],
        out_specs=(hbm, hbm, vm),
        scratch_shapes=[
            bf(OWNED, NROWS, D_ENC),
            bf(D_ENC, 2 * FEAT),
            bf(ROWS + RIM, FEAT),
            bf(ROWS + RIM, FEAT),
            pltpu.VMEM((1, 128), jnp.int32),
            pltpu.VMEM((PEERS, 1, 128), jnp.int32),
            pltpu.SMEM((PEERS, 1, 128), jnp.int32),
            bf(PEERS, HALF, D_ENC),
            bf(PEERS, NROWS, D_ENC),
            bf(PEERS, NROWS, 2 * FEAT),
            bf(PEERS, D_ENC, NROWS),
            bf(D_ENC, REFS * NROWS),
            bf(REFS, NROWS, 2 * FEAT),
            pltpu.VMEM((REFS, HALF, D_ENC), F32),
            pltpu.VMEM((REFS, HALF, D_ENC), F32),
            bf(REFS, HALF, D_ENC),
            bf(PEERS, HALF, D_ENC),
            bf(OWNED, HALF, D_ENC),
            bf(ROWS, FEAT),
            bf(RIM, FEAT),
            bf(ROWS, FEAT),
            bf(GROUPS, 2, SIDE, SIDE, SHARE, STEP),
            bf(GROUPS, SIDE - 1, SIDE, SHARE, STEP),
            bf(GROUPS, SIDE - 1, SIDE, SHARE, STEP),
            bf(GROUPS - 1, SIDE, SHARE, STEP),
            bf(GROUPS - 1, SIDE, SHARE, STEP),
            bf(SIDE - 1, GROUPS - 1, SHARE, STEP),
            bf(SIDE - 1, GROUPS - 1, SHARE, STEP),
            bf(DEPTH, 2, 8, FEAT - STEP),
            bf(DEPTH, 2, 8, FEAT - STEP),
            bf(DEPTH, 2, PEERS, 8, STEP),
            bf(DEPTH, 2, PEERS, 8, STEP),
            bf(PEERS, 2, 8, STEP),
            bf(PEERS, 2, 8, STEP),
            dma((6,)), dma((2,)),
            dma((PEERS,)), dma((PEERS,)), dma((PEERS,)), dma((PEERS,)), dma((PEERS,)), dma((PEERS,)),
            dma((2,)), dma((2,)), dma((2,)),
            dma((PEERS,)), dma((PEERS,)), dma((2,)), dma((2, GROUPS)),
            dma((GROUPS, 3)), dma((GROUPS, 3)), dma((GROUPS, 3)), dma((GROUPS, 3)),
            dma((3,)), dma((3,)), dma((3,)), dma((3,)),
            dma((DEPTH,)), dma((DEPTH,)), dma((DEPTH,)), dma((DEPTH,)), dma((PEERS,)), dma((PEERS,)),
        ],
        compiler_params=pltpu.CompilerParams(
            collective_id=0, has_side_effects=True, vmem_limit_bytes=VMEM_LIMIT
        ),
        name="spans",
    )(
        jnp.swapaxes(owner_map, 1, 2), nbr_count, encodings.reshape(OWNED, NROWS, D_ENC),
        queries[0], out_grad[0], key_weight, value_weight,
    )
    parts = (
        pl.BlockSpec((ROWS // 4, FEAT), lambda n: (n, 0)),
        pl.BlockSpec((OWNED // 4, NROWS, D_ENC), lambda n: (n, 0, 0)),
        pl.BlockSpec((PIECE, 2, FEAT), lambda n: (0, 0, 0)),
    )
    gq, ge, gw = pl.pallas_call(
        finish_kernel,
        grid=(4,),
        out_shape=tuple(jax.ShapeDtypeStruct(a.shape, a.dtype) for a in (gq, ge, gw)),
        in_specs=parts,
        out_specs=parts,
        name="finish",
    )(gq, ge, gw)
    return gq[None], ge.reshape(1, OWNED * NROWS, D_ENC), gw


def solution(mesh):
    return jax.shard_map(
        body,
        mesh=mesh,
        in_specs=(
            P("dp", "seq", "head"),
            P("dp", "seq", "head"),
            P("dp", "seq", None),
            P("dp", "seq", None),
            P("dp", "seq"),
            P(None, "head"),
            P(None, "head"),
        ),
        out_specs=(P("dp", "seq", "head"), P("dp", "seq", None), P(("seq", "dp"), None, "head")),
        check_vma=False,
    )
```
